128 devices in a mesh: snap: 8 (over x, core), bond: 16 (over y, z).
Axes of the slice: x: 4, y: 4, z: 4, core: 2. Of those that a mesh axis runs over, the one named last changes fastest.
Arguments:
- yields: bfloat16 [8192, 32768], P('snap', 'bond'), may hold values from -60 to 60
- partners: int32 [256, 16], P('bond'), may hold values from -1 to 255, as said below
Outputs:
- bond_means: float32 [32768], P('bond')
- covariance_tiles: float32 [16, 256, 128, 128], P('snap', 'bond')
The draws below stay inside these ranges and needn't reach their ends.
Inputs may be any that keep to these rules, and one draw needn't show every extreme that they name: `partners`: row i lists i first, then distinct blocks in ascending order among i + 1 to i + 56 - 1 (below 256), then -1 in the remaining slots; every row lists at least one block, and some row fills all 16 slots.
All inputs are finite; a program needn't handle non-finite values.
Results may differ from the reference program's by a relative error of at most 0.0007.
Values may be sent and summed in bfloat16 or wider, within the bound.
A program may use at most 128 MiB of HBM per device.

```python
import math
import jax
import jax.numpy as jnp
from jax import lax

BONDS = 32768
BLOCK = 128
NB = 256
REACH = 56
KMAX = 16
SNAPS = 8192


def draw_yields(key, part):
    keys = jax.random.split(key, 7)
    col_scale = jnp.exp(jax.random.uniform(keys[0], (1, BONDS), jnp.float32, math.log(0.3), math.log(3.0)))
    row_scale = jnp.exp(jax.random.uniform(keys[1], (SNAPS, 1), jnp.float32, math.log(0.5), math.log(2.0)))
    drift = jax.random.uniform(keys[2], (1, BONDS), jnp.float32, -2.0, 2.0)
    factors = jax.random.normal(keys[3], (SNAPS, 8), jnp.float32)
    loadings = jax.random.normal(keys[4], (8, BONDS), jnp.float32) * 0.35
    noise = jax.random.normal(keys[6], (SNAPS, BONDS), jnp.float32)
    common = jnp.dot(factors, loadings, precision=lax.Precision.HIGHEST)
    values = (noise + common) * row_scale * col_scale + drift * col_scale
    return jnp.clip(values, -60.0, 60.0).astype(jnp.bfloat16)


def draw_partners(key, part):
    key_order = jax.random.fold_in(key, 11)
    key_count = jax.random.fold_in(key, 12)
    key_forced = jax.random.fold_in(key, 13)
    block_ids = jnp.arange(NB, dtype=jnp.int32)[:, None]
    offsets = jnp.arange(REACH, dtype=jnp.int32)[None, :]
    scores = jax.random.randint(key_order, (NB, REACH), 0, 1 << 20) * REACH + offsets
    scores = jnp.where(offsets == 0, -1, scores)
    scores = jnp.where(block_ids + offsets >= NB, (1 << 20) * REACH + REACH, scores)
    ordering = jnp.argsort(scores, axis=1)[:, :KMAX].astype(jnp.int32)
    counts = jax.random.randint(key_count, (NB,), 1, KMAX + 1)
    forced = jax.random.randint(key_forced, (), 0, NB - REACH)
    counts = jnp.where(jnp.arange(NB) == forced, KMAX, counts)
    room_left = jnp.minimum(REACH, NB - jnp.arange(NB))
    counts = jnp.minimum(counts, room_left)
    slot_ids = jnp.arange(KMAX)[None, :]
    chosen = jnp.where(slot_ids < counts[:, None], ordering, REACH + 1)
    chosen = jnp.sort(chosen, axis=1)
    return jnp.where(chosen <= REACH - 1, block_ids + chosen, -1).astype(jnp.int32)


def setup_inputs(seed: int = 0) -> dict:
    key_list = jax.random.split(jax.random.key(seed), 3)
    return {
        "yields": draw_yields(jax.random.fold_in(key_list[2], 71), 0),
        "partners": draw_partners(jax.random.fold_in(key_list[2], 71), 0),
    }


def reference(yields, partners):
    column_sums = jnp.sum(yields, axis=0, dtype=jnp.float32)
    bond_means = column_sums / SNAPS
    centered = (yields.astype(jnp.float32) - bond_means[None, :]).astype(jnp.bfloat16)
    blocked = centered.reshape(SNAPS, NB, BLOCK)

    def per_block(args):
        block_row, partner_row = args
        own_block = lax.dynamic_index_in_dim(blocked, block_row, 1, keepdims=False).astype(jnp.float32)
        live_row = partner_row >= 0
        safe_index = jnp.where(live_row, partner_row, 0).astype(jnp.int32)
        chosen = jnp.take(blocked, safe_index, axis=1).astype(jnp.float32)
        tile_sum = jnp.einsum("sa,scb->cab", own_block, chosen, precision=lax.Precision.HIGHEST)
        return tile_sum * live_row.astype(jnp.float32)[:, None, None] / (SNAPS - 1)

    tiles = lax.map(per_block, (jnp.arange(NB, dtype=jnp.int32), partners))
    return bond_means, jnp.transpose(tiles, (1, 0, 2, 3))
```

```python
import functools

import jax
import jax.numpy as jnp
from jax import lax
from jax.experimental import pallas as pl
from jax.experimental.pallas import tpu as pltpu
from jax.sharding import PartitionSpec as P

BLOCK = 128
NB = 16
SLOTS = 16
NX = 4
NZ = 4
NY = 4
PARTIAL = 7
CHUNKS = 8
LAG_A, LAG_B, LAG_C = 1, 3, 5
MESH = pl.DeviceIdType.MESH


def kernel(
    total_snaps,
    x_ref,
    partners_ref,
    mean_ref,
    out_ref,
    ext,
    own_t,
    part,
    twin,
    hop,
    last,
    sums,
    load_sem,
    mean_send,
    mean_recv,
    col_send,
    col_recv,
    twin_send,
    twin_recv,
    hop_send,
    hop_recv,
    last_send,
    last_recv,
):
    snaps = ext.shape[1]
    rows = snaps // CHUNKS
    half = CHUNKS // 2
    snap = lax.axis_index("snap")
    bond = lax.axis_index("bond")
    chip_x, core = snap // 2, lax.rem(snap, 2)
    y, z = bond // NZ, lax.rem(bond, NZ)

    def at_x(step):
        return (lax.rem(chip_x + step + NX, NX) * 2 + core, bond)

    def at_z(step):
        return (snap, y * NZ + lax.rem(z + step + NZ, NZ))

    def at_y(step):
        return (snap, lax.rem(y + step + NY, NY) * NZ + z)

    twin_id = (chip_x * 2 + 1 - core, bond)

    barrier = pltpu.get_barrier_semaphore()
    for step in range(1, 8):
        pl.semaphore_signal(
            barrier, inc=1, device_id=(lax.rem(snap + step, 8), bond), device_id_type=MESH
        )
    for device in (at_z(1), at_z(-1), at_y(1), at_y(-1)):
        pl.semaphore_signal(barrier, inc=1, device_id=device, device_id_type=MESH)

    def own_load(block):
        return pltpu.make_async_copy(
            x_ref.at[:, pl.ds(block * BLOCK, BLOCK)], ext.at[block], load_sem.at[block]
        )

    for block in range(NB):
        own_load(block).start()
    for block in range(NB):
        own_load(block).wait()
        sums[snap, pl.ds(block, 1), :] = jnp.sum(
            ext[block].astype(jnp.float32), axis=0, keepdims=True
        )
    pl.semaphore_wait(barrier, 11)

    def mean_copy(step):
        peer = lax.rem(snap + step, 8)
        return pltpu.make_async_remote_copy(
            src_ref=sums.at[snap],
            dst_ref=sums.at[snap],
            send_sem=mean_send.at[step],
            recv_sem=mean_recv.at[snap],
            device_id=(peer, bond),
            device_id_type=MESH,
        )

    def mean_arrival(step):
        peer = lax.rem(snap + step, 8)
        return pltpu.make_async_remote_copy(
            src_ref=sums.at[peer],
            dst_ref=sums.at[peer],
            send_sem=mean_send.at[step],
            recv_sem=mean_recv.at[peer],
            device_id=(peer, bond),
            device_id_type=MESH,
        )

    for step in range(1, 8):
        mean_copy(step).start()
    for step in range(1, 8):
        mean_arrival(step).wait_recv()
    for step in range(1, 8):
        mean_copy(step).wait_send()
    means = jnp.sum(sums[...], axis=0) / total_snaps
    mean_ref[...] = means

    @pl.loop(0, NB)
    def _(block):
        mean = mean_ref[pl.ds(block, 1), :]
        ext[block] = (ext[block].astype(jnp.float32) - mean).astype(jnp.bfloat16)

    def send(direction, index, source, target, count, chunk, device):
        return pltpu.make_async_remote_copy(
            src_ref=ext.at[pl.ds(source * NB, count), pl.ds(chunk * rows, rows)],
            dst_ref=ext.at[pl.ds(target * NB, count), pl.ds(chunk * rows, rows)],
            send_sem=col_send.at[direction, index],
            recv_sem=col_recv.at[target, chunk],
            device_id=device,
            device_id_type=MESH,
        )

    def arrive(target, chunk, count=NB):
        send(0, 0, target, target, count, chunk, at_z(1)).wait_recv()

    y_count = jnp.where(z == NZ - 1, PARTIAL, NB)
    second_minus = jnp.where(z == 0, 5, 2)
    second_plus = jnp.where(z == NZ - 1, 5, 2)

    def y_own(n, count):
        chunk = lax.rem(n + half, CHUNKS)
        return send(0, n, 0, 4, count, chunk, at_y(-1))

    def minus_own(n):
        chunk = lax.rem(n + half, CHUNKS)
        return send(1, n, 0, 1, NB, chunk, at_z(-1))

    def minus_forward(n):
        chunk = lax.rem(n + half, CHUNKS)
        return send(1, n, 4, 1, NB, chunk, at_z(-1))

    def minus_second(j):
        return send(1, CHUNKS + j, 1, second_minus, NB, half + j, at_z(-1))

    def plus_own(n):
        return send(2, n, 0, 3, NB, n, at_z(1))

    def plus_forward(n):
        chunk = lax.rem(n + half, CHUNKS)
        return send(2, n, 4, 3, NB, chunk, at_z(1))

    def plus_second(j):
        return send(2, CHUNKS + j, 3, second_plus, NB, j, at_z(1))

    def relay_up(j):
        return send(3, j, 5, 2, NB, j, at_y(1))

    def relay_down(j):
        return send(3, j, 5, 2, NB, half + j, at_y(-1))

    first, final = z == 0, z == NZ - 1

    @pl.loop(0, CHUNKS)
    def _(n):
        @pl.when(jnp.logical_not(final))
        def _():
            y_own(n, NB).start()

        @pl.when(jnp.logical_not(first))
        def _():
            minus_own(n).start()

        @pl.when(final)
        def _():
            plus_own(n).start()
            y_own(n, PARTIAL).start()

    @pl.loop(0, NB)
    def _(block):
        own_t[block] = jnp.transpose(ext[block])

    @pl.loop(0, half)
    def _(j):
        @pl.when(jnp.logical_not(final))
        def _():
            arrive(4, half + j)
            plus_forward(j).start()

        @pl.when(first)
        def _():
            minus_forward(j).start()
            arrive(1, half + j)
            minus_second(j).start()

        @pl.when(final)
        def _():
            arrive(1, half + j)
            minus_second(j).start()
            arrive(5, half + j)
            relay_down(j).start()
            arrive(3, j)
            plus_second(j).start()

    @pl.when(jnp.logical_not(final))
    def _():
        @pl.loop(half, CHUNKS)
        def _(n):
            arrive(4, n - half)
            plus_forward(n).start()

            @pl.when(first)
            def _():
                minus_forward(n).start()

        @pl.loop(0, half)
        def _(j):
            @pl.when(jnp.logical_not(first))
            def _():
                arrive(1, half + j)
                minus_second(j).start()

            arrive(3, j)
            plus_second(j).start()

    @pl.when(first)
    def _():
        @pl.loop(0, half)
        def _(j):
            arrive(5, j)
            relay_up(j).start()

    @pl.loop(0, half)
    def _(j):
        arrive(1, j)
        arrive(3, half + j)
        arrive(2, j)
        arrive(2, half + j)

    @pl.when(final)
    def _():
        @pl.loop(0, CHUNKS)
        def _(n):
            arrive(4, n, PARTIAL)

    owner_far = lax.rem(chip_x + 2, NX)
    owner_plus = lax.rem(chip_x + 1, NX)
    owner_minus = lax.rem(chip_x + 3, NX)
    first_block = bond * NB
    inverse = 1.0 / (total_snaps - 1)

    def twin_copy(row):
        return pltpu.make_async_remote_copy(
            src_ref=part.at[row, 1 - core],
            dst_ref=twin.at[row],
            send_sem=twin_send.at[row],
            recv_sem=twin_recv.at[row],
            device_id=twin_id,
            device_id_type=MESH,
        )

    def hop_copy(row, way):
        return pltpu.make_async_remote_copy(
            src_ref=part.at[row, core, owner_far, way],
            dst_ref=hop.at[row, way],
            send_sem=hop_send.at[row, way],
            recv_sem=hop_recv.at[row, way],
            device_id=at_x(1 - 2 * way),
            device_id_type=MESH,
        )

    def last_copy(row, way):
        return pltpu.make_async_remote_copy(
            src_ref=part.at[row, core, owner_minus if way else owner_plus],
            dst_ref=last.at[row, way],
            send_sem=last_send.at[row, way],
            recv_sem=last_recv.at[row, way],
            device_id=at_x(1 - 2 * way),
            device_id_type=MESH,
        )

    @pl.loop(0, NB + LAG_C)
    def _(t):
        @pl.when(t < NB)
        def _():
            lhs = own_t[t]
            for pair in range(SLOTS // 2):
                chosen = []
                for j in range(2):
                    partner = partners_ref[t, 2 * pair + j]
                    index = jnp.clip(partner - first_block, 0, 5 * NB - 1)
                    chosen.append(ext[index])
                tiles = jnp.dot(
                    lhs, jnp.concatenate(chosen, axis=1), preferred_element_type=jnp.float32
                )
                part[t, pair % 2, pair // 2, 0] = tiles[:, :BLOCK]
                part[t, pair % 2, pair // 2, 1] = tiles[:, BLOCK:]
            twin_copy(t).start()

        @pl.when(jnp.logical_and(t >= LAG_A, t < NB + LAG_A))
        def _():
            row = t - LAG_A
            twin_copy(row).wait_recv()
            part[row, core] += twin[row]
            hop_copy(row, 0).start()
            hop_copy(row, 1).start()

        @pl.when(jnp.logical_and(t >= LAG_B, t < NB + LAG_B))
        def _():
            row = t - LAG_B
            hop_copy(row, 0).wait_recv()
            part[row, core, owner_plus, 0] += hop[row, 0]
            last_copy(row, 0).start()
            hop_copy(row, 1).wait_recv()
            part[row, core, owner_minus, 1] += hop[row, 1]
            last_copy(row, 1).start()

        @pl.when(t >= LAG_C)
        def _():
            row = t - LAG_C
            last_copy(row, 0).wait_recv()
            last_copy(row, 1).wait_recv()
            for j in range(2):
                live = partners_ref[row, 2 * snap + j] >= 0
                scale = jnp.where(live, jnp.float32(inverse), jnp.float32(0.0))
                out_ref[j, row] = scale * (
                    part[row, core, chip_x, j] + last[row, 0, j] + last[row, 1, j]
                )

    @pl.loop(0, NB)
    def _(row):
        twin_copy(row).wait_send()
        for way in range(2):
            hop_copy(row, way).wait_send()
            last_copy(row, way).wait_send()

    @pl.loop(0, CHUNKS)
    def _(n):
        minus_own(n).wait_send()
        plus_own(n).wait_send()

        @pl.when(final)
        def _():
            y_own(n, PARTIAL).wait_send()

        @pl.when(jnp.logical_not(final))
        def _():
            y_own(n, NB).wait_send()

    @pl.loop(0, half)
    def _(j):
        minus_second(j).wait_send()
        plus_second(j).wait_send()

        @pl.when(first)
        def _():
            relay_up(j).wait_send()

        @pl.when(final)
        def _():
            relay_down(j).wait_send()


def shards(yields, partners):
    snaps, columns = yields.shape
    total_snaps = snaps * lax.axis_size("snap")
    tile = (BLOCK, BLOCK)
    f32, bf16 = jnp.float32, jnp.bfloat16
    dma = pltpu.SemaphoreType.DMA
    means, tiles = pl.pallas_call(
        functools.partial(kernel, total_snaps),
        out_shape=(
            jax.ShapeDtypeStruct((NB, BLOCK), f32),
            jax.ShapeDtypeStruct((2, NB) + tile, f32),
        ),
        in_specs=[
            pl.BlockSpec(memory_space=pl.ANY),
            pl.BlockSpec(memory_space=pltpu.SMEM),
        ],
        out_specs=(
            pl.BlockSpec(memory_space=pltpu.VMEM),
            pl.BlockSpec(memory_space=pltpu.VMEM),
        ),
        scratch_shapes=[
            pltpu.VMEM((6 * NB, snaps, BLOCK), bf16),
            pltpu.VMEM((NB, BLOCK, snaps), bf16),
            pltpu.VMEM((NB, 2, NX, 2) + tile, f32),
            pltpu.VMEM((NB, NX, 2) + tile, f32),
            pltpu.VMEM((NB, 2) + tile, f32),
            pltpu.VMEM((NB, 2, 2) + tile, f32),
            pltpu.VMEM((8, NB, BLOCK), f32),
            dma((NB,)),
            dma((8,)),
            dma((8,)),
            dma((4, CHUNKS + CHUNKS // 2)),
            dma((6, CHUNKS)),
            dma((NB,)),
            dma((NB,)),
            dma((NB, 2)),
            dma((NB, 2)),
            dma((NB, 2)),
            dma((NB, 2)),
        ],
        compiler_params=pltpu.CompilerParams(
            collective_id=0, has_side_effects=True, vmem_limit_bytes=67_000_000
        ),
    )(yields, partners)
    return means.reshape(columns), tiles


def solution(mesh):
    return jax.shard_map(
        shards,
        mesh=mesh,
        in_specs=(P("snap", "bond"), P("bond", None)),
        out_specs=(P("bond"), P("snap", "bond", None, None)),
        check_vma=False,
    )
```

```python
import functools

import jax
import jax.numpy as jnp
from jax import lax
from jax.experimental import pallas as pl
from jax.experimental.pallas import tpu as pltpu
from jax.sharding import PartitionSpec as P

BLOCK = 128
NB = 16
SLOTS = 16
NX = 4
NZ = 4
NY = 4
PARTIAL = 7
CHUNKS = 16
LAG_A, LAG_B, LAG_C = 1, 3, 5
MESH = pl.DeviceIdType.MESH


def kernel(
    total_snaps,
    x_ref,
    partners_ref,
    mean_ref,
    out_ref,
    ext,
    own_t,
    part,
    twin,
    hop,
    last,
    sums,
    means,
    load_sem,
    sum_send,
    sum_recv,
    mean_send,
    mean_recv,
    col_send,
    col_recv,
    twin_send,
    twin_recv,
    hop_send,
    hop_recv,
    last_send,
    last_recv,
):
    snaps = ext.shape[1]
    rows = snaps // CHUNKS
    half = CHUNKS // 2
    snap = lax.axis_index("snap")
    bond = lax.axis_index("bond")
    chip_x, core = snap // 2, lax.rem(snap, 2)
    y, z = bond // NZ, lax.rem(bond, NZ)

    def at_x(step):
        return (lax.rem(chip_x + step + NX, NX) * 2 + core, bond)

    def at_z(step):
        return (snap, y * NZ + lax.rem(z + step + NZ, NZ))

    def at_y(step):
        return (snap, lax.rem(y + step + NY, NY) * NZ + z)

    def at_bond(step):
        return (snap, lax.rem(bond + step + NY * NZ, NY * NZ))

    twin_id = (chip_x * 2 + 1 - core, bond)

    barrier = pltpu.get_barrier_semaphore()
    for step in range(1, 8):
        pl.semaphore_signal(
            barrier, inc=1, device_id=(lax.rem(snap + step, 8), bond), device_id_type=MESH
        )
    for step in range(-4, 5):
        if step:
            pl.semaphore_signal(
                barrier, inc=1, device_id=at_bond(step), device_id_type=MESH
            )

    def own_load(block):
        return pltpu.make_async_copy(
            x_ref.at[:, pl.ds(block * BLOCK, BLOCK)], ext.at[block], load_sem.at[block]
        )

    for block in range(NB):
        own_load(block).start()
    for block in range(NB):
        own_load(block).wait()
    pl.semaphore_wait(barrier, 15)

    def sum_copy(step, source):
        return pltpu.make_async_remote_copy(
            src_ref=sums.at[source],
            dst_ref=sums.at[source],
            send_sem=sum_send.at[step],
            recv_sem=sum_recv.at[source],
            device_id=(lax.rem(snap + step, 8), bond),
            device_id_type=MESH,
        )

    def mean_copy(step):
        return pltpu.make_async_remote_copy(
            src_ref=means.at[pl.ds(0, NB)],
            dst_ref=means.at[pl.ds(step * NB, NB)],
            send_sem=mean_send.at[step],
            recv_sem=mean_recv.at[step],
            device_id=at_bond(-step),
            device_id_type=MESH,
        )

    def send(direction, index, source, target, count, chunk, device):
        return pltpu.make_async_remote_copy(
            src_ref=ext.at[pl.ds(source * NB, count), pl.ds(chunk * rows, rows)],
            dst_ref=ext.at[pl.ds(target * NB, count), pl.ds(chunk * rows, rows)],
            send_sem=col_send.at[direction, index],
            recv_sem=col_recv.at[target, chunk],
            device_id=device,
            device_id_type=MESH,
        )

    def arrive(target, chunk, count=NB):
        send(0, 0, target, target, count, chunk, at_z(1)).wait_recv()

    y_count = jnp.where(z == NZ - 1, PARTIAL, NB)
    second_minus = jnp.where(z == 0, 5, 2)
    second_plus = jnp.where(z == NZ - 1, 5, 2)

    def y_own(n, count):
        chunk = lax.rem(n + half, CHUNKS)
        return send(0, n, 0, 4, count, chunk, at_y(-1))

    def minus_own(n):
        chunk = lax.rem(n + half, CHUNKS)
        return send(1, n, 0, 1, NB, chunk, at_z(-1))

    def minus_forward(n):
        chunk = lax.rem(n + half, CHUNKS)
        return send(1, n, 4, 1, NB, chunk, at_z(-1))

    def minus_second(j):
        return send(1, CHUNKS + j, 1, second_minus, NB, half + j, at_z(-1))

    def plus_own(n):
        return send(2, n, 0, 3, NB, n, at_z(1))

    def plus_forward(n):
        chunk = lax.rem(n + half, CHUNKS)
        return send(2, n, 4, 3, NB, chunk, at_z(1))

    def plus_second(j):
        return send(2, CHUNKS + j, 3, second_plus, NB, j, at_z(1))

    def relay_up(j):
        return send(3, j, 5, 2, NB, j, at_y(1))

    def relay_down(j):
        return send(3, j, 5, 2, NB, half + j, at_y(-1))

    first, final = z == 0, z == NZ - 1

    @pl.loop(0, CHUNKS)
    def _(n):
        @pl.when(jnp.logical_not(final))
        def _():
            y_own(n, NB).start()

        @pl.when(jnp.logical_not(first))
        def _():
            minus_own(n).start()

        @pl.when(final)
        def _():
            plus_own(n).start()
            y_own(n, PARTIAL).start()

    for block in range(NB):
        sums[snap, pl.ds(block, 1), :] = jnp.sum(
            ext[block].astype(jnp.float32), axis=0, keepdims=True
        )
    for step in range(1, 8):
        sum_copy(step, snap).start()

    @pl.loop(0, half)
    def _(j):
        @pl.when(jnp.logical_not(final))
        def _():
            arrive(4, half + j)
            plus_forward(j).start()

        @pl.when(first)
        def _():
            minus_forward(j).start()
            arrive(1, half + j)
            minus_second(j).start()

        @pl.when(final)
        def _():
            arrive(1, half + j)
            minus_second(j).start()
            arrive(5, half + j)
            relay_down(j).start()
            arrive(3, j)
            plus_second(j).start()

    for step in range(1, 8):
        sum_copy(step, lax.rem(snap + step, 8)).wait_recv()
    total = sums[0]
    for shard in range(1, 8):
        total += sums[shard]
    mean_ref[...] = total / total_snaps
    for block in range(NB):
        means[block] = mean_ref[pl.ds(block, 1), :]
    for step in range(1, 5):
        mean_copy(step).start()

    def centered(block):
        return (ext[block].astype(jnp.float32) - means[block]).astype(jnp.bfloat16)

    @pl.loop(half, CHUNKS)
    def _(n):
        @pl.when(jnp.logical_not(final))
        def _():
            arrive(4, n - half)
            plus_forward(n).start()

        @pl.when(first)
        def _():
            minus_forward(n).start()

        for each in range(NB // half):
            block = (n - half) * (NB // half) + each
            own_t[block] = jnp.transpose(centered(block))

    @pl.when(jnp.logical_not(final))
    def _():
        @pl.loop(0, half)
        def _(j):
            @pl.when(jnp.logical_not(first))
            def _():
                arrive(1, half + j)
                minus_second(j).start()

            arrive(3, j)
            plus_second(j).start()

    @pl.when(first)
    def _():
        @pl.loop(0, half)
        def _(j):
            arrive(5, j)
            relay_up(j).start()

    @pl.loop(0, half)
    def _(j):
        arrive(1, j)
        arrive(3, half + j)
        arrive(2, j)
        arrive(2, half + j)

    @pl.when(final)
    def _():
        @pl.loop(0, CHUNKS)
        def _(n):
            arrive(4, n, PARTIAL)

    for step in range(1, 5):
        mean_copy(step).wait_recv()

    owner_far = lax.rem(chip_x + 2, NX)
    owner_plus = lax.rem(chip_x + 1, NX)
    owner_minus = lax.rem(chip_x + 3, NX)
    first_block = bond * NB
    inverse = 1.0 / (total_snaps - 1)

    def twin_copy(row):
        return pltpu.make_async_remote_copy(
            src_ref=part.at[row, 1 - core],
            dst_ref=twin.at[row],
            send_sem=twin_send.at[row],
            recv_sem=twin_recv.at[row],
            device_id=twin_id,
            device_id_type=MESH,
        )

    def hop_copy(row, way):
        return pltpu.make_async_remote_copy(
            src_ref=part.at[row, core, owner_far, way],
            dst_ref=hop.at[row, way],
            send_sem=hop_send.at[row, way],
            recv_sem=hop_recv.at[row, way],
            device_id=at_x(1 - 2 * way),
            device_id_type=MESH,
        )

    def last_copy(row, way):
        return pltpu.make_async_remote_copy(
            src_ref=part.at[row, core, owner_minus if way else owner_plus],
            dst_ref=last.at[row, way],
            send_sem=last_send.at[row, way],
            recv_sem=last_recv.at[row, way],
            device_id=at_x(1 - 2 * way),
            device_id_type=MESH,
        )

    @pl.loop(0, NB + LAG_C)
    def _(t):
        @pl.when(t < NB)
        def _():
            lhs = own_t[t]
            for pair in range(SLOTS // 2):
                chosen = []
                for j in range(2):
                    partner = partners_ref[t, 2 * pair + j]
                    index = jnp.clip(partner - first_block, 0, 5 * NB - 1)
                    chosen.append(centered(index))
                tiles = jnp.dot(
                    lhs, jnp.concatenate(chosen, axis=1), preferred_element_type=jnp.float32
                )
                part[t, pair % 2, pair // 2, 0] = tiles[:, :BLOCK]
                part[t, pair % 2, pair // 2, 1] = tiles[:, BLOCK:]
            twin_copy(t).start()

        @pl.when(jnp.logical_and(t >= LAG_A, t < NB + LAG_A))
        def _():
            row = t - LAG_A
            twin_copy(row).wait_recv()
            part[row, core] += twin[row]
            hop_copy(row, 0).start()
            hop_copy(row, 1).start()

        @pl.when(jnp.logical_and(t >= LAG_B, t < NB + LAG_B))
        def _():
            row = t - LAG_B
            hop_copy(row, 0).wait_recv()
            part[row, core, owner_plus, 0] += hop[row, 0]
            last_copy(row, 0).start()
            hop_copy(row, 1).wait_recv()
            part[row, core, owner_minus, 1] += hop[row, 1]
            last_copy(row, 1).start()

        @pl.when(t >= LAG_C)
        def _():
            row = t - LAG_C
            last_copy(row, 0).wait_recv()
            last_copy(row, 1).wait_recv()
            for j in range(2):
                live = partners_ref[row, 2 * snap + j] >= 0
                scale = jnp.where(live, jnp.float32(inverse), jnp.float32(0.0))
                out_ref[j, row] = scale * (
                    part[row, core, chip_x, j] + last[row, 0, j] + last[row, 1, j]
                )

    for step in range(1, 8):
        sum_copy(step, snap).wait_send()
    for step in range(1, 5):
        mean_copy(step).wait_send()

    @pl.loop(0, NB)
    def _(row):
        twin_copy(row).wait_send()
        for way in range(2):
            hop_copy(row, way).wait_send()
            last_copy(row, way).wait_send()

    @pl.loop(0, CHUNKS)
    def _(n):
        minus_own(n).wait_send()
        plus_own(n).wait_send()

        @pl.when(final)
        def _():
            y_own(n, PARTIAL).wait_send()

        @pl.when(jnp.logical_not(final))
        def _():
            y_own(n, NB).wait_send()

    @pl.loop(0, half)
    def _(j):
        minus_second(j).wait_send()
        plus_second(j).wait_send()

        @pl.when(first)
        def _():
            relay_up(j).wait_send()

        @pl.when(final)
        def _():
            relay_down(j).wait_send()


def shards(yields, partners):
    snaps, columns = yields.shape
    total_snaps = snaps * lax.axis_size("snap")
    tile = (BLOCK, BLOCK)
    f32, bf16 = jnp.float32, jnp.bfloat16
    dma = pltpu.SemaphoreType.DMA
    bond_means, tiles = pl.pallas_call(
        functools.partial(kernel, total_snaps),
        out_shape=(
            jax.ShapeDtypeStruct((NB, BLOCK), f32),
            jax.ShapeDtypeStruct((2, NB) + tile, f32),
        ),
        in_specs=[
            pl.BlockSpec(memory_space=pl.ANY),
            pl.BlockSpec(memory_space=pltpu.SMEM),
        ],
        out_specs=(
            pl.BlockSpec(memory_space=pltpu.VMEM),
            pl.BlockSpec(memory_space=pltpu.VMEM),
        ),
        scratch_shapes=[
            pltpu.VMEM((6 * NB, snaps, BLOCK), bf16),
            pltpu.VMEM((NB, BLOCK, snaps), bf16),
            pltpu.VMEM((NB, 2, NX, 2) + tile, f32),
            pltpu.VMEM((NB, NX, 2) + tile, f32),
            pltpu.VMEM((NB, 2) + tile, f32),
            pltpu.VMEM((NB, 2, 2) + tile, f32),
            pltpu.VMEM((8, NB, BLOCK), f32),
            pltpu.VMEM((5 * NB, 1, BLOCK), f32),
            dma((NB,)),
            dma((8,)),
            dma((8,)),
            dma((5,)),
            dma((5,)),
            dma((4, CHUNKS + CHUNKS // 2)),
            dma((6, CHUNKS)),
            dma((NB,)),
            dma((NB,)),
            dma((NB, 2)),
            dma((NB, 2)),
            dma((NB, 2)),
            dma((NB, 2)),
        ],
        compiler_params=pltpu.CompilerParams(
            collective_id=0, has_side_effects=True, vmem_limit_bytes=67_000_000
        ),
    )(yields, partners)
    return bond_means.reshape(columns), tiles


def solution(mesh):
    return jax.shard_map(
        shards,
        mesh=mesh,
        in_specs=(P("snap", "bond"), P("bond", None)),
        out_specs=(P("bond"), P("snap", "bond", None, None)),
        check_vma=False,
    )
```

```python
import functools

import jax
import jax.numpy as jnp
from jax import lax
from jax.experimental import pallas as pl
from jax.experimental.pallas import tpu as pltpu
from jax.sharding import PartitionSpec as P

BLOCK = 128
NB = 16
SLOTS = 16
NX = 4
NZ = 4
NY = 4
PARTIAL = 7
CHUNKS = 16
LOW = NB // 2
EARLY = 5
LATER = CHUNKS - EARLY
DIRECT = 2
LAG_A, LAG_B, LAG_C = 1, 2, 4
PLUS_LAG, MINUS_LAG, RELAY_LAG = 2, 4, 5
MEANS_AT = 2
MESH = pl.DeviceIdType.MESH


def kernel(
    total_snaps,
    x_ref,
    partners_ref,
    mean_ref,
    out_ref,
    ext,
    late,
    own_t,
    part,
    twin,
    hop,
    last,
    sums,
    means,
    load_sem,
    sum_send,
    sum_recv,
    mean_send,
    mean_recv,
    col_send,
    col_recv,
    twin_send,
    twin_recv,
    hop_send,
    hop_recv,
    last_send,
    last_recv,
    late_recv,
):
    snaps = ext.shape[1]
    rows = snaps // CHUNKS
    snap = lax.axis_index("snap")
    bond = lax.axis_index("bond")
    chip_x, core = snap // 2, lax.rem(snap, 2)
    y, z = bond // NZ, lax.rem(bond, NZ)

    def at_x(step):
        return (lax.rem(chip_x + step + NX, NX) * 2 + core, bond)

    def at_z(step):
        return (snap, y * NZ + lax.rem(z + step + NZ, NZ))

    def at_y(step):
        return (snap, lax.rem(y + step + NY, NY) * NZ + z)

    def at_bond(step):
        return (snap, lax.rem(bond + step + NY * NZ, NY * NZ))

    twin_id = (chip_x * 2 + 1 - core, bond)

    barrier = pltpu.get_barrier_semaphore()
    for step in range(1, 8):
        pl.semaphore_signal(
            barrier, inc=1, device_id=(lax.rem(snap + step, 8), bond), device_id_type=MESH
        )
    for step in range(-4, 5):
        if step:
            pl.semaphore_signal(
                barrier, inc=1, device_id=at_bond(step), device_id_type=MESH
            )

    def own_load(block):
        return pltpu.make_async_copy(
            x_ref.at[:, pl.ds(block * BLOCK, BLOCK)], ext.at[block], load_sem.at[block]
        )

    for block in range(NB):
        own_load(block).start()
    for block in range(NB):
        own_load(block).wait()
    pl.semaphore_wait(barrier, 15)

    def sum_copy(step, source):
        return pltpu.make_async_remote_copy(
            src_ref=sums.at[source],
            dst_ref=sums.at[source],
            send_sem=sum_send.at[step],
            recv_sem=sum_recv.at[source],
            device_id=(lax.rem(snap + step, 8), bond),
            device_id_type=MESH,
        )

    def mean_copy(step):
        return pltpu.make_async_remote_copy(
            src_ref=means.at[pl.ds(0, NB)],
            dst_ref=means.at[pl.ds(step * NB, NB)],
            send_sem=mean_send.at[step],
            recv_sem=mean_recv.at[step],
            device_id=at_bond(-step),
            device_id_type=MESH,
        )

    whole, lower, upper, some = (0, NB), (0, LOW), (LOW, LOW), (0, PARTIAL)
    first, final = z == 0, z == NZ - 1
    ahead = jnp.where(final, 0, 4)
    behind = jnp.where(first, 4, 0)
    second_minus = jnp.where(first, 5, 2)
    second_plus = jnp.where(final, 5, 2)
    UPPER_2 = 0

    def upper_order(n):
        return lax.rem(n + EARLY, CHUNKS)

    def send(direction, index, source, target, blocks, chunk, device, arrival=None):
        start, count = blocks
        return pltpu.make_async_remote_copy(
            src_ref=ext.at[pl.ds(source * NB + start, count), pl.ds(chunk * rows, rows)],
            dst_ref=ext.at[pl.ds(target * NB + start, count), pl.ds(chunk * rows, rows)],
            send_sem=col_send.at[direction, index],
            recv_sem=col_recv.at[target if arrival is None else arrival, chunk],
            device_id=device,
            device_id_type=MESH,
        )

    def arrive(target, chunk, blocks=whole, arrival=None):
        send(0, 0, target, target, blocks, chunk, at_z(1), arrival).wait_recv()

    def either(n, act):
        @pl.when(n < EARLY)
        def _():
            act(whole)

        @pl.when(n >= EARLY)
        def _():
            act(lower)

    def y_own(n, blocks):
        return send(0, n, 0, 4, blocks, n, at_y(-1))

    def minus_primary(n):
        chunk = jnp.where(first, n, upper_order(n))
        return send(1, n, behind, 1, whole, chunk, at_z(-1))

    def direct(n):
        return send(1, n, 0, 5, whole, n, at_z(-1))

    def direct_down(n):
        return send(3, LATER + n, 5, 1, whole, n, at_y(-1))

    def minus_second(n):
        arrival = jnp.where(first, 5, UPPER_2)
        return send(1, CHUNKS + n, 1, second_minus, upper, EARLY + n, at_z(-1), arrival)

    def plus_primary(n, blocks):
        return send(2, n, ahead, 3, blocks, n, at_z(1))

    def plus_second(n, blocks):
        return send(2, CHUNKS + n, 3, second_plus, blocks, n, at_z(1))

    def relay_up(n, blocks):
        return send(3, n, 5, 2, blocks, n, at_y(1))

    def relay_down(n):
        return send(3, n, 5, 2, upper, EARLY + n, at_y(-1), UPPER_2)

    def plus_late(block):
        return pltpu.make_async_remote_copy(
            src_ref=ext.at[ahead * NB + LOW + block, pl.ds(EARLY * rows, LATER * rows)],
            dst_ref=late.at[block],
            send_sem=col_send.at[2, 2 * CHUNKS + block],
            recv_sem=late_recv.at[block],
            device_id=at_z(1),
            device_id_type=MESH,
        )

    @pl.loop(0, CHUNKS)
    def _(n):
        @pl.when(jnp.logical_not(final))
        def _():
            y_own(n, whole).start()

        @pl.when(jnp.logical_not(first))
        def _():
            minus_primary(n).start()

        @pl.when(jnp.logical_and(first, n < DIRECT))
        def _():
            direct(n).start()

        @pl.when(final)
        def _():
            y_own(n, some).start()

            @pl.when(n < 2)
            def _():
                plus_primary(n, whole).start()

    def centered(block):
        return (ext[block].astype(jnp.float32) - means[block]).astype(jnp.bfloat16)

    def forward(n):
        @pl.when(jnp.logical_and(n < CHUNKS, jnp.logical_not(final)))
        def _():
            arrive(4, n)
            either(n, lambda blocks: plus_primary(n, blocks).start())

        @pl.when(jnp.logical_and(n < CHUNKS, first))
        def _():
            @pl.when(n >= DIRECT)
            def _():
                minus_primary(n).start()

            @pl.when(n < LATER)
            def _():
                arrive(1, EARLY + n)
                minus_second(n).start()

        @pl.when(jnp.logical_and(n < CHUNKS - 2, final))
        def _():
            either(n + 2, lambda blocks: plus_primary(n + 2, blocks).start())

        @pl.when(jnp.logical_and(n >= PLUS_LAG, n < CHUNKS + PLUS_LAG))
        def _():
            m = n - PLUS_LAG

            def act(blocks):
                arrive(3, m, blocks)
                plus_second(m, blocks).start()

            either(m, act)

        middle = jnp.logical_not(jnp.logical_or(first, final))

        @pl.when(jnp.logical_and(middle, jnp.logical_and(n >= MINUS_LAG, n < LATER + MINUS_LAG)))
        def _():
            m = n - MINUS_LAG
            arrive(1, EARLY + m)
            minus_second(m).start()

        m_down = n - n // 3
        m_second = m_down - EARLY
        turn = jnp.logical_and(final, lax.rem(n, 3) != 2)

        @pl.when(jnp.logical_and(final, n < DIRECT))
        def _():
            arrive(5, n)
            direct_down(n).start()

        @pl.when(jnp.logical_and(turn, m_down < LATER))
        def _():
            arrive(5, EARLY + m_down, upper)
            relay_down(m_down).start()

        @pl.when(jnp.logical_and(turn, jnp.logical_and(m_second >= 0, m_second < LATER)))
        def _():
            arrive(1, EARLY + m_second)
            minus_second(m_second).start()

        @pl.when(jnp.logical_and(first, jnp.logical_and(n >= RELAY_LAG, n < CHUNKS + RELAY_LAG)))
        def _():
            m = n - RELAY_LAG

            def act(blocks):
                arrive(5, m, blocks)
                relay_up(m, blocks).start()

            either(m, act)

    @pl.loop(0, MEANS_AT)
    def _(n):
        forward(n)

    for block in range(NB):
        sums[snap, pl.ds(block, 1), :] = jnp.sum(
            ext[block].astype(jnp.float32), axis=0, keepdims=True
        )
    for step in range(1, 8):
        sum_copy(step, snap).start()
    for step in range(1, 8):
        sum_copy(step, lax.rem(snap + step, 8)).wait_recv()
    total = sums[0]
    for shard in range(1, 8):
        total += sums[shard]
    mean_ref[...] = total / total_snaps
    for block in range(NB):
        means[block] = mean_ref[pl.ds(block, 1), :]
    for step in range(1, 5):
        mean_copy(step).start()

    @pl.loop(MEANS_AT, CHUNKS + CHUNKS // 2)
    def _(n):
        forward(n)

        @pl.when(n - MEANS_AT < NB)
        def _():
            own_t[n - MEANS_AT] = jnp.transpose(centered(n - MEANS_AT))

    @pl.loop(0, LOW)
    def _(block):
        plus_late(block).start()

    @pl.loop(0, EARLY)
    def _(n):
        arrive(2, n)
        arrive(1, n)

    @pl.loop(EARLY, CHUNKS)
    def _(n):
        arrive(2, n, lower)
        arrive(2, n, upper, UPPER_2)

    @pl.when(final)
    def _():
        @pl.loop(0, CHUNKS)
        def _(n):
            arrive(4, n, some)

    for step in range(1, 5):
        mean_copy(step).wait_recv()

    owner_far = lax.rem(chip_x + 2, NX)
    owner_plus = lax.rem(chip_x + 1, NX)
    owner_minus = lax.rem(chip_x + 3, NX)
    first_block = bond * NB
    inverse = 1.0 / (total_snaps - 1)

    def twin_copy(row):
        return pltpu.make_async_remote_copy(
            src_ref=part.at[row, 1 - core],
            dst_ref=twin.at[row],
            send_sem=twin_send.at[row],
            recv_sem=twin_recv.at[row],
            device_id=twin_id,
            device_id_type=MESH,
        )

    def hop_copy(row, way):
        return pltpu.make_async_remote_copy(
            src_ref=part.at[row, core, owner_far, way],
            dst_ref=hop.at[row, way],
            send_sem=hop_send.at[row, way],
            recv_sem=hop_recv.at[row, way],
            device_id=at_x(1 - 2 * way),
            device_id_type=MESH,
        )

    def last_copy(row, way):
        return pltpu.make_async_remote_copy(
            src_ref=part.at[row, core, owner_minus if way else owner_plus],
            dst_ref=last.at[row, way],
            send_sem=last_send.at[row, way],
            recv_sem=last_recv.at[row, way],
            device_id=at_x(1 - 2 * way),
            device_id_type=MESH,
        )

    @pl.loop(0, NB + LAG_C)
    def _(t):
        @pl.when(jnp.logical_and(t >= 1, t <= LOW))
        def _():
            plus_late(t - 1).wait_recv()
            ext[3 * NB + LOW - 1 + t, pl.ds(EARLY * rows, LATER * rows)] = late[t - 1]

        @pl.when(t < NB)
        def _():
            lhs = own_t[t]
            for pair in range(SLOTS // 2):
                chosen = []
                for j in range(2):
                    partner = partners_ref[t, 2 * pair + j]
                    index = jnp.clip(partner - first_block, 0, 5 * NB - 1)
                    chosen.append(centered(index))
                tiles = jnp.dot(
                    lhs, jnp.concatenate(chosen, axis=1), preferred_element_type=jnp.float32
                )
                part[t, pair % 2, pair // 2, 0] = tiles[:, :BLOCK]
                part[t, pair % 2, pair // 2, 1] = tiles[:, BLOCK:]
            twin_copy(t).start()

        @pl.when(jnp.logical_and(t >= LAG_A, t < NB + LAG_A))
        def _():
            row = t - LAG_A
            twin_copy(row).wait_recv()
            part[row, core] += twin[row]
            hop_copy(row, 0).start()
            hop_copy(row, 1).start()

        @pl.when(jnp.logical_and(t >= LAG_B, t < NB + LAG_B))
        def _():
            row = t - LAG_B
            hop_copy(row, 0).wait_recv()
            part[row, core, owner_plus, 0] += hop[row, 0]
            last_copy(row, 0).start()
            hop_copy(row, 1).wait_recv()
            part[row, core, owner_minus, 1] += hop[row, 1]
            last_copy(row, 1).start()

        @pl.when(t >= LAG_C)
        def _():
            row = t - LAG_C
            last_copy(row, 0).wait_recv()
            last_copy(row, 1).wait_recv()
            for j in range(2):
                live = partners_ref[row, 2 * snap + j] >= 0
                scale = jnp.where(live, jnp.float32(inverse), jnp.float32(0.0))
                out_ref[j, row] = scale * (
                    part[row, core, chip_x, j] + last[row, 0, j] + last[row, 1, j]
                )

    for step in range(1, 8):
        sum_copy(step, snap).wait_send()
    for step in range(1, 5):
        mean_copy(step).wait_send()

    @pl.loop(0, NB)
    def _(row):
        twin_copy(row).wait_send()
        for way in range(2):
            hop_copy(row, way).wait_send()
            last_copy(row, way).wait_send()

    @pl.loop(0, CHUNKS)
    def _(n):
        minus_primary(n).wait_send()
        either(n, lambda blocks: plus_primary(n, blocks).wait_send())
        either(n, lambda blocks: plus_second(n, blocks).wait_send())

        @pl.when(final)
        def _():
            y_own(n, some).wait_send()

        @pl.when(jnp.logical_not(final))
        def _():
            y_own(n, whole).wait_send()

        @pl.when(n < LATER)
        def _():
            minus_second(n).wait_send()

        @pl.when(first)
        def _():
            either(n, lambda blocks: relay_up(n, blocks).wait_send())

        @pl.when(jnp.logical_and(final, n < LATER))
        def _():
            relay_down(n).wait_send()

        @pl.when(jnp.logical_and(final, n < DIRECT))
        def _():
            direct_down(n).wait_send()

    @pl.loop(0, LOW)
    def _(block):
        plus_late(block).wait_send()


def shards(yields, partners):
    snaps, columns = yields.shape
    total_snaps = snaps * lax.axis_size("snap")
    tile = (BLOCK, BLOCK)
    f32, bf16 = jnp.float32, jnp.bfloat16
    dma = pltpu.SemaphoreType.DMA
    bond_means, tiles = pl.pallas_call(
        functools.partial(kernel, total_snaps),
        out_shape=(
            jax.ShapeDtypeStruct((NB, BLOCK), f32),
            jax.ShapeDtypeStruct((2, NB) + tile, f32),
        ),
        in_specs=[
            pl.BlockSpec(memory_space=pl.ANY),
            pl.BlockSpec(memory_space=pltpu.SMEM),
        ],
        out_specs=(
            pl.BlockSpec(memory_space=pltpu.VMEM),
            pl.BlockSpec(memory_space=pltpu.VMEM),
        ),
        scratch_shapes=[
            pltpu.VMEM((6 * NB, snaps, BLOCK), bf16),
            pltpu.VMEM((LOW, snaps * LATER // CHUNKS, BLOCK), bf16),
            pltpu.VMEM((NB, BLOCK, snaps), bf16),
            pltpu.VMEM((NB, 2, NX, 2) + tile, f32),
            pltpu.VMEM((NB, NX, 2) + tile, f32),
            pltpu.VMEM((NB, 2) + tile, f32),
            pltpu.VMEM((NB, 2, 2) + tile, f32),
            pltpu.VMEM((8, NB, BLOCK), f32),
            pltpu.VMEM((5 * NB, 1, BLOCK), f32),
            dma((NB,)),
            dma((8,)),
            dma((8,)),
            dma((5,)),
            dma((5,)),
            dma((4, 2 * CHUNKS + LOW)),
            dma((6, CHUNKS)),
            dma((NB,)),
            dma((NB,)),
            dma((NB, 2)),
            dma((NB, 2)),
            dma((NB, 2)),
            dma((NB, 2)),
            dma((LOW,)),
        ],
        compiler_params=pltpu.CompilerParams(
            collective_id=0, has_side_effects=True, vmem_limit_bytes=67_000_000
        ),
    )(yields, partners)
    return bond_means.reshape(columns), tiles


def solution(mesh):
    return jax.shard_map(
        shards,
        mesh=mesh,
        in_specs=(P("snap", "bond"), P("bond", None)),
        out_specs=(P("bond"), P("snap", "bond", None, None)),
        check_vma=False,
    )
```

```python
import functools

import jax
import jax.numpy as jnp
from jax import lax
from jax.experimental import pallas as pl
from jax.experimental.pallas import tpu as pltpu
from jax.sharding import PartitionSpec as P

BLOCK = 128
NB = 16
SLOTS = 16
NX = 4
NZ = 4
NY = 4
PARTIAL = 7
CHUNKS = 16
LOW = NB // 2
EARLY = 5
LATER = CHUNKS - EARLY
DIRECT = 2
LAG_A, LAG_B, LAG_C = 1, 2, 4
PLUS_LAG, MINUS_LAG, RELAY_LAG = 2, 4, 5
MEANS_AT = 2
MESH = pl.DeviceIdType.MESH


def kernel(
    total_snaps,
    x_ref,
    partners_ref,
    mean_ref,
    out_ref,
    ext,
    late,
    own_t,
    part,
    twin,
    hop,
    last,
    sums,
    means,
    load_sem,
    sum_send,
    sum_recv,
    mean_send,
    mean_recv,
    col_send,
    col_recv,
    twin_send,
    twin_recv,
    hop_send,
    hop_recv,
    last_send,
    last_recv,
    late_recv,
):
    snaps = ext.shape[1]
    rows = snaps // CHUNKS
    snap = lax.axis_index("snap")
    bond = lax.axis_index("bond")
    chip_x, core = snap // 2, lax.rem(snap, 2)
    y, z = bond // NZ, lax.rem(bond, NZ)

    def at_x(step):
        return (lax.rem(chip_x + step + NX, NX) * 2 + core, bond)

    def at_z(step):
        return (snap, y * NZ + lax.rem(z + step + NZ, NZ))

    def at_y(step):
        return (snap, lax.rem(y + step + NY, NY) * NZ + z)

    def at_bond(step):
        return (snap, lax.rem(bond + step + NY * NZ, NY * NZ))

    twin_id = (chip_x * 2 + 1 - core, bond)

    barrier = pltpu.get_barrier_semaphore()
    for step in range(1, 8):
        pl.semaphore_signal(
            barrier, inc=1, device_id=(lax.rem(snap + step, 8), bond), device_id_type=MESH
        )
    for step in range(-4, 5):
        if step:
            pl.semaphore_signal(
                barrier, inc=1, device_id=at_bond(step), device_id_type=MESH
            )

    def own_load(block):
        return pltpu.make_async_copy(
            x_ref.at[:, pl.ds(block * BLOCK, BLOCK)], ext.at[block], load_sem.at[block]
        )

    for block in range(NB):
        own_load(block).start()
    for block in range(NB):
        own_load(block).wait()
    pl.semaphore_wait(barrier, 15)

    def sum_copy(step, source):
        return pltpu.make_async_remote_copy(
            src_ref=sums.at[source],
            dst_ref=sums.at[source],
            send_sem=sum_send.at[step],
            recv_sem=sum_recv.at[source],
            device_id=(lax.rem(snap + step, 8), bond),
            device_id_type=MESH,
        )

    def mean_copy(step):
        return pltpu.make_async_remote_copy(
            src_ref=means.at[pl.ds(0, NB)],
            dst_ref=means.at[pl.ds(step * NB, NB)],
            send_sem=mean_send.at[step],
            recv_sem=mean_recv.at[step],
            device_id=at_bond(-step),
            device_id_type=MESH,
        )

    whole, lower, upper, some = (0, NB), (0, LOW), (LOW, LOW), (0, PARTIAL)
    first, final = z == 0, z == NZ - 1
    ahead = jnp.where(final, 0, 4)
    behind = jnp.where(first, 4, 0)
    second_minus = jnp.where(first, 5, 2)
    second_plus = jnp.where(final, 5, 2)
    UPPER_2 = 0

    def upper_order(n):
        return lax.rem(n + EARLY, CHUNKS)

    def send(direction, index, source, target, blocks, chunk, device, arrival=None):
        start, count = blocks
        return pltpu.make_async_remote_copy(
            src_ref=ext.at[pl.ds(source * NB + start, count), pl.ds(chunk * rows, rows)],
            dst_ref=ext.at[pl.ds(target * NB + start, count), pl.ds(chunk * rows, rows)],
            send_sem=col_send.at[direction, index],
            recv_sem=col_recv.at[target if arrival is None else arrival, chunk],
            device_id=device,
            device_id_type=MESH,
        )

    def arrive(target, chunk, blocks=whole, arrival=None):
        send(0, 0, target, target, blocks, chunk, at_z(1), arrival).wait_recv()

    def either(n, act):
        @pl.when(n < EARLY)
        def _():
            act(whole)

        @pl.when(n >= EARLY)
        def _():
            act(lower)

    def y_own(n, blocks):
        return send(0, n, 0, 4, blocks, n, at_y(-1))

    def minus_primary(n):
        chunk = jnp.where(first, n, upper_order(n))
        return send(1, n, behind, 1, whole, chunk, at_z(-1))

    def direct(n):
        return send(1, n, 0, 5, whole, n, at_z(-1))

    def direct_down(n):
        return send(3, LATER + n, 5, 1, whole, n, at_y(-1))

    def minus_second(n):
        arrival = jnp.where(first, 5, UPPER_2)
        return send(1, CHUNKS + n, 1, second_minus, upper, EARLY + n, at_z(-1), arrival)

    def plus_primary(n, blocks):
        return send(2, n, ahead, 3, blocks, n, at_z(1))

    def plus_second(n, blocks):
        return send(2, CHUNKS + n, 3, second_plus, blocks, n, at_z(1))

    def relay_up(n, blocks):
        return send(3, n, 5, 2, blocks, n, at_y(1))

    def relay_down(n):
        return send(3, n, 5, 2, upper, EARLY + n, at_y(-1), UPPER_2)

    def plus_late(block):
        return pltpu.make_async_remote_copy(
            src_ref=ext.at[ahead * NB + LOW + block, pl.ds(EARLY * rows, LATER * rows)],
            dst_ref=late.at[block],
            send_sem=col_send.at[2, 2 * CHUNKS + block],
            recv_sem=late_recv.at[block],
            device_id=at_z(1),
            device_id_type=MESH,
        )

    @pl.loop(0, CHUNKS)
    def _(n):
        @pl.when(jnp.logical_not(final))
        def _():
            y_own(n, whole).start()

        @pl.when(jnp.logical_not(first))
        def _():
            minus_primary(n).start()

        @pl.when(jnp.logical_and(first, n < DIRECT))
        def _():
            direct(n).start()

        @pl.when(final)
        def _():
            y_own(n, some).start()

            @pl.when(n < 2)
            def _():
                plus_primary(n, whole).start()

    def centered(block):
        return (ext[block].astype(jnp.float32) - means[block]).astype(jnp.bfloat16)

    def forward(n):
        @pl.when(jnp.logical_and(n < CHUNKS, jnp.logical_not(final)))
        def _():
            arrive(4, n)
            either(n, lambda blocks: plus_primary(n, blocks).start())

        @pl.when(jnp.logical_and(n < CHUNKS, first))
        def _():
            @pl.when(n >= DIRECT)
            def _():
                minus_primary(n).start()

            @pl.when(n < LATER)
            def _():
                arrive(1, EARLY + n)
                minus_second(n).start()

        @pl.when(jnp.logical_and(n < CHUNKS - 2, final))
        def _():
            either(n + 2, lambda blocks: plus_primary(n + 2, blocks).start())

        @pl.when(jnp.logical_and(n >= PLUS_LAG, n < CHUNKS + PLUS_LAG))
        def _():
            m = n - PLUS_LAG

            def act(blocks):
                arrive(3, m, blocks)
                plus_second(m, blocks).start()

            either(m, act)

        middle = jnp.logical_not(jnp.logical_or(first, final))

        @pl.when(jnp.logical_and(middle, jnp.logical_and(n >= MINUS_LAG, n < LATER + MINUS_LAG)))
        def _():
            m = n - MINUS_LAG
            arrive(1, EARLY + m)
            minus_second(m).start()

        m_down = n - n // 3
        m_second = m_down - EARLY
        turn = jnp.logical_and(final, lax.rem(n, 3) != 2)

        @pl.when(jnp.logical_and(final, n < DIRECT))
        def _():
            arrive(5, n)
            direct_down(n).start()

        @pl.when(jnp.logical_and(turn, m_down < LATER))
        def _():
            arrive(5, EARLY + m_down, upper)
            relay_down(m_down).start()

        @pl.when(jnp.logical_and(turn, jnp.logical_and(m_second >= 0, m_second < LATER)))
        def _():
            arrive(1, EARLY + m_second)
            minus_second(m_second).start()

        @pl.when(jnp.logical_and(first, jnp.logical_and(n >= RELAY_LAG, n < CHUNKS + RELAY_LAG)))
        def _():
            m = n - RELAY_LAG

            def act(blocks):
                arrive(5, m, blocks)
                relay_up(m, blocks).start()

            either(m, act)

    @pl.loop(0, MEANS_AT)
    def _(n):
        forward(n)

    for block in range(NB):
        sums[snap, pl.ds(block, 1), :] = jnp.sum(
            ext[block].astype(jnp.float32), axis=0, keepdims=True
        )
    for step in range(1, 8):
        sum_copy(step, snap).start()
    for step in range(1, 8):
        sum_copy(step, lax.rem(snap + step, 8)).wait_recv()
    total = sums[0]
    for shard in range(1, 8):
        total += sums[shard]
    mean_ref[...] = total / total_snaps
    for block in range(NB):
        means[block] = mean_ref[pl.ds(block, 1), :]
    for step in range(1, 5):
        mean_copy(step).start()

    @pl.loop(MEANS_AT, CHUNKS + CHUNKS // 2)
    def _(n):
        forward(n)

        @pl.when(n - MEANS_AT < NB)
        def _():
            own_t[n - MEANS_AT] = jnp.transpose(centered(n - MEANS_AT))

    @pl.loop(0, LOW)
    def _(block):
        plus_late(block).start()

    @pl.loop(0, EARLY)
    def _(n):
        arrive(2, n)
        arrive(1, n)

    @pl.loop(EARLY, CHUNKS)
    def _(n):
        arrive(2, n, lower)
        arrive(2, n, upper, UPPER_2)

    @pl.when(final)
    def _():
        @pl.loop(0, CHUNKS)
        def _(n):
            arrive(4, n, some)

    for step in range(1, 5):
        mean_copy(step).wait_recv()

    owner_far = lax.rem(chip_x + 2, NX)
    owner_plus = lax.rem(chip_x + 1, NX)
    owner_minus = lax.rem(chip_x + 3, NX)
    first_block = bond * NB
    inverse = 1.0 / (total_snaps - 1)

    def twin_copy(row):
        return pltpu.make_async_remote_copy(
            src_ref=part.at[row, 1 - core],
            dst_ref=twin.at[row],
            send_sem=twin_send.at[row],
            recv_sem=twin_recv.at[row],
            device_id=twin_id,
            device_id_type=MESH,
        )

    def hop_copy(row, way):
        return pltpu.make_async_remote_copy(
            src_ref=part.at[row, core, owner_far, way],
            dst_ref=hop.at[row, way],
            send_sem=hop_send.at[row, way],
            recv_sem=hop_recv.at[row, way],
            device_id=at_x(1 - 2 * way),
            device_id_type=MESH,
        )

    def last_copy(row, way):
        return pltpu.make_async_remote_copy(
            src_ref=part.at[row, core, owner_minus if way else owner_plus],
            dst_ref=last.at[row, way],
            send_sem=last_send.at[row, way],
            recv_sem=last_recv.at[row, way],
            device_id=at_x(1 - 2 * way),
            device_id_type=MESH,
        )

    @pl.loop(0, NB + LAG_C)
    def _(t):
        @pl.when(jnp.logical_and(t >= 1, t <= LOW))
        def _():
            plus_late(t - 1).wait_recv()
            ext[3 * NB + LOW - 1 + t, pl.ds(EARLY * rows, LATER * rows)] = late[t - 1]

        @pl.when(t < NB)
        def _():
            lhs = own_t[t]
            for pair in range(SLOTS // 2):
                chosen = []
                for j in range(2):
                    partner = partners_ref[t, 2 * pair + j]
                    index = jnp.clip(partner - first_block, 0, 5 * NB - 1)
                    chosen.append(centered(index))
                tiles = jnp.dot(
                    lhs, jnp.concatenate(chosen, axis=1), preferred_element_type=jnp.float32
                )
                part[t, pair % 2, pair // 2, 0] = tiles[:, :BLOCK]
                part[t, pair % 2, pair // 2, 1] = tiles[:, BLOCK:]
            twin_copy(t).start()

        @pl.when(jnp.logical_and(t >= LAG_A, t < NB + LAG_A))
        def _():
            row = t - LAG_A
            twin_copy(row).wait_recv()
            part[row, core] += twin[row]
            hop_copy(row, 0).start()
            hop_copy(row, 1).start()

        @pl.when(jnp.logical_and(t >= LAG_B, t < NB + LAG_B))
        def _():
            row = t - LAG_B
            hop_copy(row, 0).wait_recv()
            part[row, core, owner_plus, 0] += hop[row, 0]
            last_copy(row, 0).start()
            hop_copy(row, 1).wait_recv()
            part[row, core, owner_minus, 1] += hop[row, 1]
            last_copy(row, 1).start()

        @pl.when(t >= LAG_C)
        def _():
            row = t - LAG_C
            last_copy(row, 0).wait_recv()
            last_copy(row, 1).wait_recv()
            for j in range(2):
                live = partners_ref[row, 2 * snap + j] >= 0
                scale = jnp.where(live, jnp.float32(inverse), jnp.float32(0.0))
                out_ref[j, row] = scale * (
                    part[row, core, chip_x, j] + last[row, 0, j] + last[row, 1, j]
                )

    for step in range(1, 8):
        sum_copy(step, snap).wait_send()
    for step in range(1, 5):
        mean_copy(step).wait_send()

    @pl.loop(0, NB)
    def _(row):
        twin_copy(row).wait_send()
        for way in range(2):
            hop_copy(row, way).wait_send()
            last_copy(row, way).wait_send()

    @pl.loop(0, CHUNKS)
    def _(n):
        minus_primary(n).wait_send()
        either(n, lambda blocks: plus_primary(n, blocks).wait_send())
        either(n, lambda blocks: plus_second(n, blocks).wait_send())

        @pl.when(final)
        def _():
            y_own(n, some).wait_send()

        @pl.when(jnp.logical_not(final))
        def _():
            y_own(n, whole).wait_send()

        @pl.when(n < LATER)
        def _():
            minus_second(n).wait_send()

        @pl.when(first)
        def _():
            either(n, lambda blocks: relay_up(n, blocks).wait_send())

        @pl.when(jnp.logical_and(final, n < LATER))
        def _():
            relay_down(n).wait_send()

        @pl.when(jnp.logical_and(final, n < DIRECT))
        def _():
            direct_down(n).wait_send()

    @pl.loop(0, LOW)
    def _(block):
        plus_late(block).wait_send()


def shards(yields, partners):
    snaps, columns = yields.shape
    total_snaps = snaps * lax.axis_size("snap")
    tile = (BLOCK, BLOCK)
    f32, bf16 = jnp.float32, jnp.bfloat16
    dma = pltpu.SemaphoreType.DMA
    bond_means, tiles = pl.pallas_call(
        functools.partial(kernel, total_snaps),
        out_shape=(
            pltpu.VMEM((NB, BLOCK), f32),
            pltpu.VMEM((2, NB) + tile, f32),
        ),
        in_specs=[
            pl.BlockSpec(memory_space=pl.ANY),
            pl.BlockSpec(memory_space=pltpu.SMEM),
        ],
        out_specs=(
            pl.BlockSpec(memory_space=pltpu.VMEM),
            pl.BlockSpec(memory_space=pltpu.VMEM),
        ),
        scratch_shapes=[
            pltpu.VMEM((6 * NB, snaps, BLOCK), bf16),
            pltpu.VMEM((LOW, snaps * LATER // CHUNKS, BLOCK), bf16),
            pltpu.VMEM((NB, BLOCK, snaps), bf16),
            pltpu.VMEM((NB, 2, NX, 2) + tile, f32),
            pltpu.VMEM((NB, NX, 2) + tile, f32),
            pltpu.VMEM((NB, 2) + tile, f32),
            pltpu.VMEM((NB, 2, 2) + tile, f32),
            pltpu.VMEM((8, NB, BLOCK), f32),
            pltpu.VMEM((5 * NB, 1, BLOCK), f32),
            dma((NB,)),
            dma((8,)),
            dma((8,)),
            dma((5,)),
            dma((5,)),
            dma((4, 2 * CHUNKS + LOW)),
            dma((6, CHUNKS)),
            dma((NB,)),
            dma((NB,)),
            dma((NB, 2)),
            dma((NB, 2)),
            dma((NB, 2)),
            dma((NB, 2)),
            dma((LOW,)),
        ],
        compiler_params=pltpu.CompilerParams(
            collective_id=0, has_side_effects=True, vmem_limit_bytes=64_500_000
        ),
    )(yields, partners)
    return bond_means.reshape(columns), tiles


def solution(mesh):
    return jax.shard_map(
        shards,
        mesh=mesh,
        in_specs=(P("snap", "bond"), P("bond", None)),
        out_specs=(P("bond"), P("snap", "bond", None, None)),
        check_vma=False,
    )
```

```python
import functools

import jax
import jax.numpy as jnp
from jax import lax
from jax.experimental import pallas as pl
from jax.experimental.pallas import tpu as pltpu
from jax.sharding import PartitionSpec as P

BLOCK = 128
NB = 16
SLOTS = 16
NX = 4
NZ = 4
NY = 4
PARTIAL = 7
CHUNKS = 16
LOW = NB // 2
EARLY = 5
LATER = CHUNKS - EARLY
PUT_OFF = 4
SIDEWAYS = 2
DIRECT = 2
LAG_A, LAG_B, LAG_C = 1, 2, 4
PLUS_LAG, MINUS_LAG, RELAY_LAG = 2, 4, 5
MEANS_AT = 2
MESH = pl.DeviceIdType.MESH


def kernel(
    total_snaps,
    x_ref,
    partners_ref,
    mean_ref,
    out_ref,
    ext,
    late,
    own_t,
    part,
    twin,
    hop,
    last,
    sums,
    means,
    load_sem,
    sum_send,
    sum_recv,
    mean_send,
    mean_recv,
    col_send,
    col_recv,
    twin_send,
    twin_recv,
    hop_send,
    hop_recv,
    last_send,
    last_recv,
    late_recv,
):
    snaps = ext.shape[1]
    rows = snaps // CHUNKS
    snap = lax.axis_index("snap")
    bond = lax.axis_index("bond")
    chip_x, core = snap // 2, lax.rem(snap, 2)
    y, z = bond // NZ, lax.rem(bond, NZ)

    def at_x(step):
        return (lax.rem(chip_x + step + NX, NX) * 2 + core, bond)

    def at_z(step):
        return (snap, y * NZ + lax.rem(z + step + NZ, NZ))

    def at_y(step):
        return (snap, lax.rem(y + step + NY, NY) * NZ + z)

    def at_bond(step):
        return (snap, lax.rem(bond + step + NY * NZ, NY * NZ))

    twin_id = (chip_x * 2 + 1 - core, bond)

    barrier = pltpu.get_barrier_semaphore()
    for step in range(1, 8):
        pl.semaphore_signal(
            barrier, inc=1, device_id=(lax.rem(snap + step, 8), bond), device_id_type=MESH
        )
    for step in range(-4, 5):
        if step:
            pl.semaphore_signal(
                barrier, inc=1, device_id=at_bond(step), device_id_type=MESH
            )

    def own_load(block):
        return pltpu.make_async_copy(
            x_ref.at[:, pl.ds(block * BLOCK, BLOCK)], ext.at[block], load_sem.at[block]
        )

    for block in range(NB):
        own_load(block).start()
    for block in range(NB):
        own_load(block).wait()
    pl.semaphore_wait(barrier, 15)

    def sum_copy(step, source):
        return pltpu.make_async_remote_copy(
            src_ref=sums.at[source],
            dst_ref=sums.at[source],
            send_sem=sum_send.at[step],
            recv_sem=sum_recv.at[source],
            device_id=(lax.rem(snap + step, 8), bond),
            device_id_type=MESH,
        )

    def mean_copy(step):
        return pltpu.make_async_remote_copy(
            src_ref=means.at[pl.ds(0, NB)],
            dst_ref=means.at[pl.ds(step * NB, NB)],
            send_sem=mean_send.at[step],
            recv_sem=mean_recv.at[step],
            device_id=at_bond(-step),
            device_id_type=MESH,
        )

    whole, lower, upper, some = (0, NB), (0, LOW), (LOW, LOW), (0, PARTIAL)
    first, final = z == 0, z == NZ - 1
    ahead = jnp.where(final, 0, 4)
    behind = jnp.where(first, 4, 0)
    second_minus = jnp.where(first, 5, 2)
    second_plus = jnp.where(final, 5, 2)
    UPPER_2 = 0

    def upper_order(n):
        return lax.rem(n + EARLY, CHUNKS)

    def send(direction, index, source, target, blocks, chunk, device, arrival=None):
        start, count = blocks
        return pltpu.make_async_remote_copy(
            src_ref=ext.at[pl.ds(source * NB + start, count), pl.ds(chunk * rows, rows)],
            dst_ref=ext.at[pl.ds(target * NB + start, count), pl.ds(chunk * rows, rows)],
            send_sem=col_send.at[direction, index],
            recv_sem=col_recv.at[target if arrival is None else arrival, chunk],
            device_id=device,
            device_id_type=MESH,
        )

    def arrive(target, chunk, blocks=whole, arrival=None):
        send(0, 0, target, target, blocks, chunk, at_z(1), arrival).wait_recv()

    def either(n, act):
        @pl.when(n < EARLY)
        def _():
            act(whole)

        @pl.when(n >= EARLY)
        def _():
            act(lower)

    def y_own(n, blocks):
        return send(0, n, 0, 4, blocks, n, at_y(-1))

    def minus_primary(n):
        chunk = jnp.where(first, n, upper_order(n))
        return send(1, n, behind, 1, whole, chunk, at_z(-1))

    def direct(n):
        return send(1, n, 0, 5, whole, n, at_z(-1))

    def direct_down(n):
        return send(3, LATER + n, 5, 1, whole, n, at_y(-1))

    def minus_second(n):
        arrival = jnp.where(first, 5, UPPER_2)
        return send(1, CHUNKS + n, 1, second_minus, upper, EARLY + n, at_z(-1), arrival)

    def plus_primary(n, blocks):
        return send(2, n, ahead, 3, blocks, n, at_z(1))

    def plus_second(n, blocks):
        return send(2, CHUNKS + n, 3, second_plus, blocks, n, at_z(1))

    def sideways(n):
        return send(2, n, 0, 5, lower, n, at_z(1), 6)

    def sideways_down(n):
        return send(3, 2 * CHUNKS + n - (CHUNKS - SIDEWAYS), 5, 3, lower, n, at_y(-1))

    def relay_up(n, blocks):
        return send(3, n, 5, 2, blocks, n, at_y(1))

    def relay_down(n):
        return send(3, n, 5, 2, upper, EARLY + n, at_y(-1), UPPER_2)

    def plus_late(block):
        return pltpu.make_async_remote_copy(
            src_ref=ext.at[ahead * NB + LOW + block, pl.ds(EARLY * rows, LATER * rows)],
            dst_ref=late.at[block],
            send_sem=col_send.at[2, 2 * CHUNKS + block],
            recv_sem=late_recv.at[block],
            device_id=at_z(1),
            device_id_type=MESH,
        )

    @pl.loop(0, CHUNKS)
    def _(n):
        @pl.when(jnp.logical_not(final))
        def _():
            y_own(n, whole).start()

        @pl.when(jnp.logical_not(first))
        def _():
            minus_primary(n).start()

        @pl.when(jnp.logical_and(first, n < DIRECT))
        def _():
            direct(n).start()

        @pl.when(jnp.logical_and(jnp.logical_not(final), n >= CHUNKS - SIDEWAYS))
        def _():
            sideways(n).start()

        @pl.when(final)
        def _():
            y_own(n, some).start()

            @pl.when(n < 2)
            def _():
                plus_primary(n, whole).start()

    def centered(block):
        return (ext[block].astype(jnp.float32) - means[block]).astype(jnp.bfloat16)

    def forward(n):
        @pl.when(jnp.logical_and(n < CHUNKS, jnp.logical_not(final)))
        def _():
            arrive(4, n)

            @pl.when(n < CHUNKS - SIDEWAYS)
            def _():
                either(n, lambda blocks: plus_primary(n, blocks).start())

        @pl.when(jnp.logical_and(n < CHUNKS, first))
        def _():
            now = jnp.logical_or(n < PUT_OFF, n >= EARLY)

            @pl.when(jnp.logical_and(n >= DIRECT, now))
            def _():
                minus_primary(n).start()

            @pl.when(n == CHUNKS - 1)
            def _():
                for chunk in range(PUT_OFF, EARLY):
                    minus_primary(chunk).start()

            @pl.when(n < LATER)
            def _():
                arrive(1, EARLY + n)
                minus_second(n).start()

        @pl.when(jnp.logical_and(n < CHUNKS - 2, final))
        def _():
            either(n + 2, lambda blocks: plus_primary(n + 2, blocks).start())

        @pl.when(jnp.logical_and(n >= PLUS_LAG, n < CHUNKS + PLUS_LAG))
        def _():
            m = n - PLUS_LAG

            def act(blocks):
                arrive(3, m, blocks)
                plus_second(m, blocks).start()

            either(m, act)

        middle = jnp.logical_not(jnp.logical_or(first, final))

        @pl.when(jnp.logical_and(middle, jnp.logical_and(n >= MINUS_LAG, n < LATER + MINUS_LAG)))
        def _():
            m = n - MINUS_LAG
            arrive(1, EARLY + m)
            minus_second(m).start()

        m_down = n - n // 3
        m_second = m_down - EARLY
        turn = jnp.logical_and(final, lax.rem(n, 3) != 2)

        @pl.when(jnp.logical_and(jnp.logical_not(first), jnp.logical_and(n >= 2, n < 2 + SIDEWAYS)))
        def _():
            chunk = CHUNKS - SIDEWAYS + n - 2
            arrive(5, chunk, lower, 6)
            sideways_down(chunk).start()

        @pl.when(jnp.logical_and(final, n < DIRECT))
        def _():
            arrive(5, n)
            direct_down(n).start()

        @pl.when(jnp.logical_and(turn, m_down < LATER))
        def _():
            arrive(5, EARLY + m_down, upper)
            relay_down(m_down).start()

        @pl.when(jnp.logical_and(turn, jnp.logical_and(m_second >= 0, m_second < LATER)))
        def _():
            arrive(1, EARLY + m_second)
            minus_second(m_second).start()

        @pl.when(jnp.logical_and(first, jnp.logical_and(n >= RELAY_LAG, n < CHUNKS + RELAY_LAG)))
        def _():
            m = n - RELAY_LAG

            def act(blocks):
                arrive(5, m, blocks)
                relay_up(m, blocks).start()

            either(m, act)

    @pl.loop(0, MEANS_AT)
    def _(n):
        forward(n)

    for block in range(NB):
        sums[snap, pl.ds(block, 1), :] = jnp.sum(
            ext[block].astype(jnp.float32), axis=0, keepdims=True
        )
    for step in range(1, 8):
        sum_copy(step, snap).start()
    for step in range(1, 8):
        sum_copy(step, lax.rem(snap + step, 8)).wait_recv()
    total = sums[0]
    for shard in range(1, 8):
        total += sums[shard]
    mean_ref[...] = total / total_snaps
    for block in range(NB):
        means[block] = mean_ref[pl.ds(block, 1), :]
    for step in range(1, 5):
        mean_copy(step).start()

    @pl.loop(MEANS_AT, CHUNKS + CHUNKS // 2)
    def _(n):
        forward(n)

        @pl.when(n - MEANS_AT < NB)
        def _():
            own_t[n - MEANS_AT] = jnp.transpose(centered(n - MEANS_AT))

    @pl.loop(0, LOW)
    def _(block):
        plus_late(block).start()

    @pl.loop(0, EARLY)
    def _(n):
        arrive(2, n)
        arrive(1, n)

    @pl.loop(EARLY, CHUNKS)
    def _(n):
        arrive(2, n, lower)
        arrive(2, n, upper, UPPER_2)

    @pl.when(final)
    def _():
        @pl.loop(0, CHUNKS)
        def _(n):
            arrive(4, n, some)

    for step in range(1, 5):
        mean_copy(step).wait_recv()

    owner_far = lax.rem(chip_x + 2, NX)
    owner_plus = lax.rem(chip_x + 1, NX)
    owner_minus = lax.rem(chip_x + 3, NX)
    first_block = bond * NB
    inverse = 1.0 / (total_snaps - 1)

    def twin_copy(row):
        return pltpu.make_async_remote_copy(
            src_ref=part.at[row, 1 - core],
            dst_ref=twin.at[row],
            send_sem=twin_send.at[row],
            recv_sem=twin_recv.at[row],
            device_id=twin_id,
            device_id_type=MESH,
        )

    def hop_copy(row, way):
        return pltpu.make_async_remote_copy(
            src_ref=part.at[row, core, owner_far, way],
            dst_ref=hop.at[row, way],
            send_sem=hop_send.at[row, way],
            recv_sem=hop_recv.at[row, way],
            device_id=at_x(1 - 2 * way),
            device_id_type=MESH,
        )

    def last_copy(row, way):
        return pltpu.make_async_remote_copy(
            src_ref=part.at[row, core, owner_minus if way else owner_plus],
            dst_ref=last.at[row, way],
            send_sem=last_send.at[row, way],
            recv_sem=last_recv.at[row, way],
            device_id=at_x(1 - 2 * way),
            device_id_type=MESH,
        )

    @pl.loop(0, NB + LAG_C)
    def _(t):
        @pl.when(jnp.logical_and(t >= 1, t <= LOW))
        def _():
            plus_late(t - 1).wait_recv()
            ext[3 * NB + LOW - 1 + t, pl.ds(EARLY * rows, LATER * rows)] = late[t - 1]

        @pl.when(t < NB)
        def _():
            lhs = own_t[t]
            for pair in range(SLOTS // 2):
                chosen = []
                for j in range(2):
                    partner = partners_ref[t, 2 * pair + j]
                    index = jnp.clip(partner - first_block, 0, 5 * NB - 1)
                    chosen.append(centered(index))
                tiles = jnp.dot(
                    lhs, jnp.concatenate(chosen, axis=1), preferred_element_type=jnp.float32
                )
                part[t, pair % 2, pair // 2, 0] = tiles[:, :BLOCK]
                part[t, pair % 2, pair // 2, 1] = tiles[:, BLOCK:]
            twin_copy(t).start()

        @pl.when(jnp.logical_and(t >= LAG_A, t < NB + LAG_A))
        def _():
            row = t - LAG_A
            twin_copy(row).wait_recv()
            part[row, core] += twin[row]
            hop_copy(row, 0).start()
            hop_copy(row, 1).start()

        @pl.when(jnp.logical_and(t >= LAG_B, t < NB + LAG_B))
        def _():
            row = t - LAG_B
            hop_copy(row, 0).wait_recv()
            part[row, core, owner_plus, 0] += hop[row, 0]
            last_copy(row, 0).start()
            hop_copy(row, 1).wait_recv()
            part[row, core, owner_minus, 1] += hop[row, 1]
            last_copy(row, 1).start()

        @pl.when(t >= LAG_C)
        def _():
            row = t - LAG_C
            last_copy(row, 0).wait_recv()
            last_copy(row, 1).wait_recv()
            for j in range(2):
                live = partners_ref[row, 2 * snap + j] >= 0
                scale = jnp.where(live, jnp.float32(inverse), jnp.float32(0.0))
                out_ref[j, row] = scale * (
                    part[row, core, chip_x, j] + last[row, 0, j] + last[row, 1, j]
                )

    for step in range(1, 8):
        sum_copy(step, snap).wait_send()
    for step in range(1, 5):
        mean_copy(step).wait_send()

    @pl.loop(0, NB)
    def _(row):
        twin_copy(row).wait_send()
        for way in range(2):
            hop_copy(row, way).wait_send()
            last_copy(row, way).wait_send()

    @pl.loop(0, CHUNKS)
    def _(n):
        minus_primary(n).wait_send()
        either(n, lambda blocks: plus_primary(n, blocks).wait_send())
        either(n, lambda blocks: plus_second(n, blocks).wait_send())

        @pl.when(final)
        def _():
            y_own(n, some).wait_send()

        @pl.when(jnp.logical_not(final))
        def _():
            y_own(n, whole).wait_send()

        @pl.when(n < LATER)
        def _():
            minus_second(n).wait_send()

        @pl.when(first)
        def _():
            either(n, lambda blocks: relay_up(n, blocks).wait_send())

        @pl.when(jnp.logical_and(final, n < LATER))
        def _():
            relay_down(n).wait_send()

        @pl.when(jnp.logical_and(final, n < DIRECT))
        def _():
            direct_down(n).wait_send()

        @pl.when(jnp.logical_and(jnp.logical_not(first), n >= CHUNKS - SIDEWAYS))
        def _():
            sideways_down(n).wait_send()

    @pl.loop(0, LOW)
    def _(block):
        plus_late(block).wait_send()


def shards(yields, partners):
    snaps, columns = yields.shape
    total_snaps = snaps * lax.axis_size("snap")
    tile = (BLOCK, BLOCK)
    f32, bf16 = jnp.float32, jnp.bfloat16
    dma = pltpu.SemaphoreType.DMA
    bond_means, tiles = pl.pallas_call(
        functools.partial(kernel, total_snaps),
        out_shape=(
            pltpu.VMEM((NB, BLOCK), f32),
            pltpu.VMEM((2, NB) + tile, f32),
        ),
        in_specs=[
            pl.BlockSpec(memory_space=pl.ANY),
            pl.BlockSpec(memory_space=pltpu.SMEM),
        ],
        out_specs=(
            pl.BlockSpec(memory_space=pltpu.VMEM),
            pl.BlockSpec(memory_space=pltpu.VMEM),
        ),
        scratch_shapes=[
            pltpu.VMEM((6 * NB, snaps, BLOCK), bf16),
            pltpu.VMEM((LOW, snaps * LATER // CHUNKS, BLOCK), bf16),
            pltpu.VMEM((NB, BLOCK, snaps), bf16),
            pltpu.VMEM((NB, 2, NX, 2) + tile, f32),
            pltpu.VMEM((NB, NX, 2) + tile, f32),
            pltpu.VMEM((NB, 2) + tile, f32),
            pltpu.VMEM((NB, 2, 2) + tile, f32),
            pltpu.VMEM((8, NB, BLOCK), f32),
            pltpu.VMEM((5 * NB, 1, BLOCK), f32),
            dma((NB,)),
            dma((8,)),
            dma((8,)),
            dma((5,)),
            dma((5,)),
            dma((4, 2 * CHUNKS + LOW)),
            dma((7, CHUNKS)),
            dma((NB,)),
            dma((NB,)),
            dma((NB, 2)),
            dma((NB, 2)),
            dma((NB, 2)),
            dma((NB, 2)),
            dma((LOW,)),
        ],
        compiler_params=pltpu.CompilerParams(
            collective_id=0, has_side_effects=True, vmem_limit_bytes=64_500_000
        ),
    )(yields, partners)
    return bond_means.reshape(columns), tiles


def solution(mesh):
    return jax.shard_map(
        shards,
        mesh=mesh,
        in_specs=(P("snap", "bond"), P("bond", None)),
        out_specs=(P("bond"), P("snap", "bond", None, None)),
        check_vma=False,
    )
```

```python
import functools

import jax
import jax.numpy as jnp
from jax import lax
from jax.experimental import pallas as pl
from jax.experimental.pallas import tpu as pltpu
from jax.sharding import PartitionSpec as P

BLOCK = 128
NB = 16
SLOTS = 16
NX = 4
NZ = 4
NY = 4
PARTIAL = 7
CHUNKS = 16
LOW = NB // 2
EARLY = 5
LATER = CHUNKS - EARLY
PUT_OFF = 4
SIDEWAYS = 2
DIRECT = 2
LAG_A, LAG_B, LAG_C = 1, 2, 4
PLUS_LAG, MINUS_LAG, RELAY_LAG = 2, 4, 5
MEANS_AT = 2
MESH = pl.DeviceIdType.MESH


def kernel(
    total_snaps,
    x_ref,
    partners_ref,
    mean_ref,
    out_ref,
    ext,
    late,
    own_t,
    part,
    twin,
    hop,
    last,
    sums,
    means,
    load_sem,
    sum_send,
    sum_recv,
    mean_send,
    mean_recv,
    col_send,
    col_recv,
    twin_send,
    twin_recv,
    hop_send,
    hop_recv,
    last_send,
    last_recv,
    late_recv,
):
    snaps = ext.shape[1]
    rows = snaps // CHUNKS
    snap = lax.axis_index("snap")
    bond = lax.axis_index("bond")
    chip_x, core = snap // 2, lax.rem(snap, 2)
    y, z = bond // NZ, lax.rem(bond, NZ)

    def at_x(step):
        return (lax.rem(chip_x + step + NX, NX) * 2 + core, bond)

    def at_z(step):
        return (snap, y * NZ + lax.rem(z + step + NZ, NZ))

    def at_y(step):
        return (snap, lax.rem(y + step + NY, NY) * NZ + z)

    def at_bond(step):
        return (snap, lax.rem(bond + step + NY * NZ, NY * NZ))

    twin_id = (chip_x * 2 + 1 - core, bond)

    barrier = pltpu.get_barrier_semaphore()
    for step in range(1, 8):
        pl.semaphore_signal(
            barrier, inc=1, device_id=(lax.rem(snap + step, 8), bond), device_id_type=MESH
        )
    for step in range(-4, 5):
        if step:
            pl.semaphore_signal(
                barrier, inc=1, device_id=at_bond(step), device_id_type=MESH
            )

    def own_load(block):
        return pltpu.make_async_copy(
            x_ref.at[:, pl.ds(block * BLOCK, BLOCK)], ext.at[block], load_sem.at[block]
        )

    for block in range(NB):
        own_load(block).start()
    for block in range(NB):
        own_load(block).wait()
    pl.semaphore_wait(barrier, 15)

    def sum_copy(step, source):
        return pltpu.make_async_remote_copy(
            src_ref=sums.at[source],
            dst_ref=sums.at[source],
            send_sem=sum_send.at[step],
            recv_sem=sum_recv.at[source],
            device_id=(lax.rem(snap + step, 8), bond),
            device_id_type=MESH,
        )

    def mean_copy(step):
        return pltpu.make_async_remote_copy(
            src_ref=means.at[pl.ds(0, NB)],
            dst_ref=means.at[pl.ds(step * NB, NB)],
            send_sem=mean_send.at[step],
            recv_sem=mean_recv.at[step],
            device_id=at_bond(-step),
            device_id_type=MESH,
        )

    whole, lower, upper, some = (0, NB), (0, LOW), (LOW, LOW), (0, PARTIAL)
    first, final = z == 0, z == NZ - 1
    ahead = jnp.where(final, 0, 4)
    behind = jnp.where(first, 4, 0)
    second_minus = jnp.where(first, 5, 2)
    second_plus = jnp.where(final, 5, 2)
    UPPER_2 = 0

    def upper_order(n):
        return lax.rem(n + EARLY, CHUNKS)

    def send(direction, index, source, target, blocks, chunk, device, arrival=None):
        start, count = blocks
        return pltpu.make_async_remote_copy(
            src_ref=ext.at[pl.ds(source * NB + start, count), pl.ds(chunk * rows, rows)],
            dst_ref=ext.at[pl.ds(target * NB + start, count), pl.ds(chunk * rows, rows)],
            send_sem=col_send.at[direction, index],
            recv_sem=col_recv.at[target if arrival is None else arrival, chunk],
            device_id=device,
            device_id_type=MESH,
        )

    def arrive(target, chunk, blocks=whole, arrival=None):
        send(0, 0, target, target, blocks, chunk, at_z(1), arrival).wait_recv()

    def either(n, act):
        @pl.when(n < EARLY)
        def _():
            act(whole)

        @pl.when(n >= EARLY)
        def _():
            act(lower)

    def y_own(n, blocks):
        return send(0, n, 0, 4, blocks, n, at_y(-1))

    def minus_primary(n):
        chunk = jnp.where(first, n, upper_order(n))
        return send(1, n, behind, 1, whole, chunk, at_z(-1))

    def direct(n):
        return send(1, n, 0, 5, whole, n, at_z(-1))

    def direct_down(n):
        return send(3, LATER + n, 5, 1, whole, n, at_y(-1))

    def minus_second(n):
        arrival = jnp.where(first, 5, UPPER_2)
        return send(1, CHUNKS + n, 1, second_minus, upper, EARLY + n, at_z(-1), arrival)

    def plus_primary(n, blocks):
        return send(2, n, ahead, 3, blocks, n, at_z(1))

    def plus_second(n, blocks):
        return send(2, CHUNKS + n, 3, second_plus, blocks, n, at_z(1))

    def sideways(n):
        return send(2, n, 0, 5, lower, n, at_z(1), 6)

    def sideways_down(n):
        return send(3, 2 * CHUNKS + n - (CHUNKS - SIDEWAYS), 5, 3, lower, n, at_y(-1))

    def relay_up(n, blocks):
        return send(3, n, 5, 2, blocks, n, at_y(1))

    def relay_down(n):
        return send(3, n, 5, 2, upper, EARLY + n, at_y(-1), UPPER_2)

    def plus_late(block):
        return pltpu.make_async_remote_copy(
            src_ref=ext.at[ahead * NB + LOW + block, pl.ds(EARLY * rows, LATER * rows)],
            dst_ref=late.at[block],
            send_sem=col_send.at[2, 2 * CHUNKS + block],
            recv_sem=late_recv.at[block],
            device_id=at_z(1),
            device_id_type=MESH,
        )

    @pl.loop(0, CHUNKS)
    def _(n):
        @pl.when(jnp.logical_not(final))
        def _():
            y_own(n, whole).start()

        @pl.when(jnp.logical_not(first))
        def _():
            minus_primary(n).start()

        @pl.when(jnp.logical_and(first, n < DIRECT))
        def _():
            direct(n).start()

        @pl.when(jnp.logical_and(jnp.logical_not(final), n >= CHUNKS - SIDEWAYS))
        def _():
            sideways(n).start()

        @pl.when(final)
        def _():
            y_own(n, some).start()

            @pl.when(n < 2)
            def _():
                plus_primary(n, whole).start()

    def centered(block):
        return (ext[block].astype(jnp.float32) - means[block]).astype(jnp.bfloat16)

    def forward(n):
        @pl.when(jnp.logical_and(n < CHUNKS, jnp.logical_not(final)))
        def _():
            arrive(4, n)

            @pl.when(n < CHUNKS - SIDEWAYS)
            def _():
                either(n, lambda blocks: plus_primary(n, blocks).start())

        @pl.when(jnp.logical_and(n < CHUNKS, first))
        def _():
            now = jnp.logical_or(n < PUT_OFF, n >= EARLY)

            @pl.when(jnp.logical_and(n >= DIRECT, now))
            def _():
                minus_primary(n).start()

            @pl.when(n == CHUNKS - 1)
            def _():
                for chunk in range(PUT_OFF, EARLY):
                    minus_primary(chunk).start()

            @pl.when(n < LATER)
            def _():
                arrive(1, EARLY + n)
                minus_second(n).start()

        @pl.when(jnp.logical_and(n < CHUNKS - 2, final))
        def _():
            either(n + 2, lambda blocks: plus_primary(n + 2, blocks).start())

        @pl.when(jnp.logical_and(n >= PLUS_LAG, n < CHUNKS + PLUS_LAG))
        def _():
            m = n - PLUS_LAG

            def act(blocks):
                arrive(3, m, blocks)
                plus_second(m, blocks).start()

            either(m, act)

        middle = jnp.logical_not(jnp.logical_or(first, final))

        @pl.when(jnp.logical_and(middle, jnp.logical_and(n >= MINUS_LAG, n < LATER + MINUS_LAG)))
        def _():
            m = n - MINUS_LAG
            arrive(1, EARLY + m)
            minus_second(m).start()

        m_down = n - n // 3
        m_second = m_down - EARLY
        turn = jnp.logical_and(final, lax.rem(n, 3) != 2)

        @pl.when(jnp.logical_and(jnp.logical_not(first), jnp.logical_and(n >= 2, n < 2 + SIDEWAYS)))
        def _():
            chunk = CHUNKS - SIDEWAYS + n - 2
            arrive(5, chunk, lower, 6)
            sideways_down(chunk).start()

        @pl.when(jnp.logical_and(final, n < DIRECT))
        def _():
            arrive(5, n)
            direct_down(n).start()

        @pl.when(jnp.logical_and(turn, m_down < LATER))
        def _():
            arrive(5, EARLY + m_down, upper)
            relay_down(m_down).start()

        @pl.when(jnp.logical_and(turn, jnp.logical_and(m_second >= 0, m_second < LATER)))
        def _():
            arrive(1, EARLY + m_second)
            minus_second(m_second).start()

        @pl.when(jnp.logical_and(first, jnp.logical_and(n >= RELAY_LAG, n < CHUNKS + RELAY_LAG)))
        def _():
            m = n - RELAY_LAG

            def act(blocks):
                arrive(5, m, blocks)
                relay_up(m, blocks).start()

            either(m, act)

    @pl.loop(0, MEANS_AT)
    def _(n):
        forward(n)

    for block in range(NB):
        sums[snap, pl.ds(block, 1), :] = jnp.sum(
            ext[block].astype(jnp.float32), axis=0, keepdims=True
        )
    for step in range(1, 8):
        sum_copy(step, snap).start()
    for step in range(1, 8):
        sum_copy(step, lax.rem(snap + step, 8)).wait_recv()
    total = sums[0]
    for shard in range(1, 8):
        total += sums[shard]
    mean_ref[...] = total / total_snaps
    for block in range(NB):
        means[block] = mean_ref[pl.ds(block, 1), :]
    for step in range(1, 5):
        mean_copy(step).start()

    @pl.loop(MEANS_AT, CHUNKS + CHUNKS // 2)
    def _(n):
        forward(n)

        @pl.when(n - MEANS_AT < NB)
        def _():
            own_t[n - MEANS_AT] = jnp.transpose(centered(n - MEANS_AT))

    @pl.loop(0, LOW)
    def _(block):
        plus_late(block).start()

    @pl.loop(0, EARLY)
    def _(n):
        arrive(2, n)
        arrive(1, n)

    @pl.loop(EARLY, CHUNKS)
    def _(n):
        arrive(2, n, lower)
        arrive(2, n, upper, UPPER_2)

    @pl.when(final)
    def _():
        @pl.loop(0, CHUNKS)
        def _(n):
            arrive(4, n, some)

    for step in range(1, 5):
        mean_copy(step).wait_recv()

    owner_far = lax.rem(chip_x + 2, NX)
    owner_plus = lax.rem(chip_x + 1, NX)
    owner_minus = lax.rem(chip_x + 3, NX)
    first_block = bond * NB
    inverse = 1.0 / (total_snaps - 1)

    def twin_copy(row):
        return pltpu.make_async_remote_copy(
            src_ref=part.at[row, 1 - core],
            dst_ref=twin.at[row],
            send_sem=twin_send.at[row],
            recv_sem=twin_recv.at[row],
            device_id=twin_id,
            device_id_type=MESH,
        )

    def hop_copy(row, way):
        return pltpu.make_async_remote_copy(
            src_ref=part.at[row, core, owner_far, way],
            dst_ref=hop.at[row, way],
            send_sem=hop_send.at[row, way],
            recv_sem=hop_recv.at[row, way],
            device_id=at_x(1 - 2 * way),
            device_id_type=MESH,
        )

    def last_copy(row, way):
        return pltpu.make_async_remote_copy(
            src_ref=part.at[row, core, owner_minus if way else owner_plus],
            dst_ref=last.at[row, way],
            send_sem=last_send.at[row, way],
            recv_sem=last_recv.at[row, way],
            device_id=at_x(1 - 2 * way),
            device_id_type=MESH,
        )

    def columns_left():
        for step in range(1, 8):
            sum_copy(step, snap).wait_send()
        for step in range(1, 5):
            mean_copy(step).wait_send()

        @pl.loop(0, CHUNKS)
        def _(n):
            minus_primary(n).wait_send()
            either(n, lambda blocks: plus_primary(n, blocks).wait_send())
            either(n, lambda blocks: plus_second(n, blocks).wait_send())

            @pl.when(final)
            def _():
                y_own(n, some).wait_send()

            @pl.when(jnp.logical_not(final))
            def _():
                y_own(n, whole).wait_send()

            @pl.when(n < LATER)
            def _():
                minus_second(n).wait_send()

            @pl.when(first)
            def _():
                either(n, lambda blocks: relay_up(n, blocks).wait_send())

            @pl.when(jnp.logical_and(final, n < LATER))
            def _():
                relay_down(n).wait_send()

            @pl.when(jnp.logical_and(final, n < DIRECT))
            def _():
                direct_down(n).wait_send()

            @pl.when(jnp.logical_and(jnp.logical_not(first), n >= CHUNKS - SIDEWAYS))
            def _():
                sideways_down(n).wait_send()

        @pl.loop(0, LOW)
        def _(block):
            plus_late(block).wait_send()

    @pl.loop(0, NB + LAG_C)
    def _(t):
        @pl.when(jnp.logical_and(t >= 1, t <= LOW))
        def _():
            plus_late(t - 1).wait_recv()
            ext[3 * NB + LOW - 1 + t, pl.ds(EARLY * rows, LATER * rows)] = late[t - 1]

        @pl.when(t < NB)
        def _():
            lhs = own_t[t]
            for pair in range(SLOTS // 2):
                chosen = []
                for j in range(2):
                    partner = partners_ref[t, 2 * pair + j]
                    index = jnp.clip(partner - first_block, 0, 5 * NB - 1)
                    chosen.append(centered(index))
                tiles = jnp.dot(
                    lhs, jnp.concatenate(chosen, axis=1), preferred_element_type=jnp.float32
                )
                part[t, pair % 2, pair // 2, 0] = tiles[:, :BLOCK]
                part[t, pair % 2, pair // 2, 1] = tiles[:, BLOCK:]
            twin_copy(t).start()

        @pl.when(jnp.logical_and(t >= LAG_A, t < NB + LAG_A))
        def _():
            row = t - LAG_A
            twin_copy(row).wait_recv()
            part[row, core] += twin[row]
            hop_copy(row, 0).start()
            hop_copy(row, 1).start()

        @pl.when(jnp.logical_and(t >= LAG_B, t < NB + LAG_B))
        def _():
            row = t - LAG_B
            hop_copy(row, 0).wait_recv()
            part[row, core, owner_plus, 0] += hop[row, 0]
            last_copy(row, 0).start()
            hop_copy(row, 1).wait_recv()
            part[row, core, owner_minus, 1] += hop[row, 1]
            last_copy(row, 1).start()

        @pl.when(t == NB - 3)
        def _():
            columns_left()

        @pl.when(t >= LAG_C)
        def _():
            row = t - LAG_C
            last_copy(row, 0).wait_recv()
            last_copy(row, 1).wait_recv()
            twin_copy(row).wait_send()
            hop_copy(row, 0).wait_send()
            hop_copy(row, 1).wait_send()
            for j in range(2):
                live = partners_ref[row, 2 * snap + j] >= 0
                scale = jnp.where(live, jnp.float32(inverse), jnp.float32(0.0))
                out_ref[j, row] = scale * (
                    part[row, core, chip_x, j] + last[row, 0, j] + last[row, 1, j]
                )

    @pl.loop(0, NB)
    def _(row):
        for way in range(2):
            last_copy(row, way).wait_send()


def shards(yields, partners):
    snaps, columns = yields.shape
    total_snaps = snaps * lax.axis_size("snap")
    tile = (BLOCK, BLOCK)
    f32, bf16 = jnp.float32, jnp.bfloat16
    dma = pltpu.SemaphoreType.DMA
    bond_means, tiles = pl.pallas_call(
        functools.partial(kernel, total_snaps),
        out_shape=(
            pltpu.VMEM((NB, BLOCK), f32),
            pltpu.VMEM((2, NB) + tile, f32),
        ),
        in_specs=[
            pl.BlockSpec(memory_space=pl.ANY),
            pl.BlockSpec(memory_space=pltpu.SMEM),
        ],
        out_specs=(
            pl.BlockSpec(memory_space=pltpu.VMEM),
            pl.BlockSpec(memory_space=pltpu.VMEM),
        ),
        scratch_shapes=[
            pltpu.VMEM((6 * NB, snaps, BLOCK), bf16),
            pltpu.VMEM((LOW, snaps * LATER // CHUNKS, BLOCK), bf16),
            pltpu.VMEM((NB, BLOCK, snaps), bf16),
            pltpu.VMEM((NB, 2, NX, 2) + tile, f32),
            pltpu.VMEM((NB, NX, 2) + tile, f32),
            pltpu.VMEM((NB, 2) + tile, f32),
            pltpu.VMEM((NB, 2, 2) + tile, f32),
            pltpu.VMEM((8, NB, BLOCK), f32),
            pltpu.VMEM((5 * NB, 1, BLOCK), f32),
            dma((NB,)),
            dma((8,)),
            dma((8,)),
            dma((5,)),
            dma((5,)),
            dma((4, 2 * CHUNKS + LOW)),
            dma((7, CHUNKS)),
            dma((NB,)),
            dma((NB,)),
            dma((NB, 2)),
            dma((NB, 2)),
            dma((NB, 2)),
            dma((NB, 2)),
            dma((LOW,)),
        ],
        compiler_params=pltpu.CompilerParams(
            collective_id=0, has_side_effects=True, vmem_limit_bytes=64_500_000
        ),
    )(yields, partners)
    return bond_means.reshape(columns), tiles


def solution(mesh):
    return jax.shard_map(
        shards,
        mesh=mesh,
        in_specs=(P("snap", "bond"), P("bond", None)),
        out_specs=(P("bond"), P("snap", "bond", None, None)),
        check_vma=False,
    )
```
